512 devices in a mesh: member: 64 (over z, x), space: 8 (over y, core).
Axes of the slice: x: 4, y: 4, z: 16, core: 2. Of those that a mesh axis runs over, the one named last changes fastest.
Arguments:
- sample_group: float32 [512, 3, 256, 256], P('member', None, 'space'), may hold values from -6 to 6
- spreading_ratio: float32 [256, 256], P('space'), may hold values from 0.04 to 0.15
- flow_ratio: float32 [256, 256], P('space'), may hold values from 0.1 to 0.35
- measured_quantity: float32 [3, 256, 256], P(None, 'space'), may hold values from -16 to 16
- measured_confidence: float32 [3, 256, 256], P(None, 'space'), may hold values from 0.1 to 1
- obs_mask: int32 [3, 256, 256], P(None, 'space'), may hold values 0 or 1
- radius: int32 [3], replicated, may hold values from 1 to 4, as said below
- temper: int32 [256], P('space'), may hold values from 0 to 3
Outputs:
- analysis: float32 [512, 3, 256, 256], P('member', None, 'space')
The draws below stay inside these ranges and needn't reach their ends.
Inputs may be any that keep to these rules, and one draw needn't show every extreme that they name: One radius a field; at least one of them equals 4.
All inputs are finite; a program needn't handle non-finite values. No bound on the sum of `obs_mask` on one device may be relied on, other than what follows from the above.
Results may differ from the reference program's by a relative error of at most 0.0003.
Values sent between devices are 32-bit elements; how exact they have to be, the bound alone decides.
No kernel may reach another device: no remote copies, remote signals or barrier semaphores. Data moves between devices by JAX's collectives and lax.ppermute only.
A program may use at most 64 MiB of HBM per device.

```python
import math
import jax
import jax.numpy as jnp
from jax import lax

ENSEMBLE_SLICE = 8
COLS = 256
STEPS = 4
RADIUS = 4
MEMBERS = 512
NROWS = 256
N_MEMBER = 64


def draw_measured_quantity(key, part):
    base_key = jax.random.fold_in(key, 11)
    noise_key = jax.random.fold_in(base_key, 0)
    values = jnp.clip(jax.random.normal(noise_key, (3, NROWS, COLS), jnp.float32), -4.0, 4.0)
    return values


def draw_radius(key, part):
    base_key = jax.random.fold_in(key, 23)
    first_key, second_key = jax.random.split(base_key)
    drawn_radii = jax.random.randint(first_key, (3,), 1, RADIUS + 1)
    chosen = jax.random.randint(second_key, (), 0, 3)
    return jnp.where(jnp.arange(3) == chosen, RADIUS, drawn_radii).astype(jnp.int32)


def place_ends(values, own_key, low, high):
    shape = values.shape
    index_at = [jax.random.randint(jax.random.fold_in(own_key, axis), (), 0, shape[axis]) for axis in range(len(shape))]
    values = values.at[tuple(index_at)].set(low)
    longest = shape.index(max(shape))
    index_at[longest] = (index_at[longest] + 1) % shape[longest]
    return values.at[tuple(index_at)].set(high)


def steps_of(own_key, shape, shards, low, high):
    factor_of, own = 1.0, jax.random.fold_in(own_key, 6)
    for axis_at, parts in shards:
        draws = jnp.exp(jax.random.uniform(jax.random.fold_in(own, axis_at), (parts,), jnp.float32, low / len(shards), high / len(shards)))
        factor_of = factor_of * jnp.repeat(draws, shape[axis_at] // parts).reshape([-1 if axis == axis_at else 1 for axis in range(len(shape))])
    return factor_of


def normal_values(own_key, dims, scale, bound, cuts=(), held_as=jnp.bfloat16):
    drawn = scale * jax.random.normal(own_key, dims, jnp.float32)
    if cuts:
        drawn = drawn * steps_of(own_key, dims, cuts, -0.22, 0.18)
    return jnp.clip(drawn, -bound, bound).astype(held_as)


def setup_inputs(seed: int = 0) -> dict:
    streams_of = jax.random.split(jax.random.key(seed), 9)
    sample_group = normal_values(streams_of[0], (MEMBERS, 3, NROWS, COLS), 1.0, 6.0, ((0, 64), (2, 8)), jnp.float32)
    spreading_ratio = jnp.clip(0.04 + 0.11000001 * jax.random.uniform(streams_of[1], (NROWS, COLS), jnp.float32) ** steps_of(streams_of[1], (NROWS, COLS), ((0, 8),), -0.2, 0.2), 0.04, 0.15)
    flow_ratio = jnp.clip(0.1 + 0.25 * jax.random.uniform(streams_of[2], (NROWS, COLS), jnp.float32) ** steps_of(streams_of[2], (NROWS, COLS), ((0, 8),), -0.2, 0.2), 0.1, 0.35)
    measured_quantity = draw_measured_quantity(jax.random.fold_in(streams_of[8], 71), 0)
    measured_confidence = jnp.clip(jnp.exp(math.log(1.0) - 2.3025851 * jax.random.uniform(streams_of[4], (3, NROWS, COLS), jnp.float32) ** steps_of(streams_of[4], (3, NROWS, COLS), ((1, 8),), -0.2, 0.2)), 0.1, 1.0)
    obs_mask = place_ends((jax.random.randint(streams_of[5], (3, NROWS, COLS), 0, 4) < 1).astype(jnp.int32), jax.random.fold_in(streams_of[5], 1), 0, 1)
    radius = draw_radius(jax.random.fold_in(streams_of[8], 71), 0)
    temper = place_ends(jax.random.randint(streams_of[7], (NROWS,), 0, 4), jax.random.fold_in(streams_of[7], 1), 0, 3).astype(jnp.int32)
    return {"sample_group": sample_group, "spreading_ratio": spreading_ratio, "flow_ratio": flow_ratio, "measured_quantity": measured_quantity, "measured_confidence": measured_confidence, "obs_mask": obs_mask, "radius": radius, "temper": temper}


jitter = 0.05
pair_list = ((0, 0), (1, 0), (1, 1), (2, 0), (2, 1), (2, 2))

def advance(field, spreading_ratio, flow_ratio):
    above = jnp.roll(field, 1, axis=-2)
    below = jnp.roll(field, -1, axis=-2)
    spread = above + below + jnp.roll(field, 1, axis=-1) + jnp.roll(field, -1, axis=-1) - 4.0 * field
    return field + spreading_ratio * spread - flow_ratio * (field - above)

def smooth(values, nearby_patch, reduce_axis):
    accumulated = jnp.zeros_like(values)
    for position in range(2 * RADIUS + 1):
        accumulated = accumulated + nearby_patch[position][:, None, None] * jnp.roll(values, position - RADIUS, axis=reduce_axis)
    return accumulated

def cholesky_rows(matrix):
    first = jnp.sqrt(matrix[0])
    second = matrix[1] / first
    fourth = matrix[3] / first
    third = jnp.sqrt(matrix[2] - second * second)
    fifth = (matrix[4] - fourth * second) / third
    sixth = jnp.sqrt(matrix[5] - fourth * fourth - fifth * fifth)
    return [first, second, third, fourth, fifth, sixth]

def lower_inverse(packed):
    head = 1.0 / packed[0]
    middle = 1.0 / packed[2]
    tail = 1.0 / packed[5]
    below_head = -packed[1] * head * middle
    below_middle = -packed[4] * middle * tail
    corner = -(packed[3] * head + packed[4] * below_head) * tail
    return [head, below_head, middle, corner, below_middle, tail]

def lower_product(left_side, right_side):
    return [left_side[0] * right_side[0], left_side[1] * right_side[0] + left_side[2] * right_side[1], left_side[2] * right_side[2], left_side[3] * right_side[0] + left_side[4] * right_side[1] + left_side[5] * right_side[3], left_side[4] * right_side[2] + left_side[5] * right_side[4], left_side[5] * right_side[5]]

def transform(updated_center, post_cov, background_center, prior_cov):
    blend_matrix_lines = lower_product(cholesky_rows(post_cov), lower_inverse(cholesky_rows(prior_cov)))
    neighbor_shifts = []
    for target_row in range(3):
        running = updated_center[target_row]
        for source in range(target_row + 1):
            running = running - blend_matrix_lines[target_row * (target_row + 1) // 2 + source] * background_center[source]
        neighbor_shifts.append(running)
    return (neighbor_shifts, blend_matrix_lines)

def correct_by_blend(field, neighbor_shifts, blend_matrix_lines):
    outputs = []
    for target_row in range(3):
        running = neighbor_shifts[target_row]
        for source in range(target_row + 1):
            running = running + blend_matrix_lines[target_row * (target_row + 1) // 2 + source] * field[:, source]
        outputs.append(running)
    return jnp.stack(outputs, axis=1)

def with_jitter(terms, divisor):
    result_list = []
    for number in range(6):
        entry = terms[number] / divisor
        if number in (0, 2, 5):
            entry = entry + jitter
        result_list.append(entry)
    return result_list

def reference(sample_group, spreading_ratio, flow_ratio, measured_quantity, measured_confidence, obs_mask, radius, temper):

    def propagate_sample(sample_position):
        for repeat in range(STEPS):
            sample_position = advance(sample_position, spreading_ratio, flow_ratio)
        return sample_position
    propagate_group = lax.map(propagate_sample, sample_group)
    nearby_patch = (jnp.abs(jnp.arange(-RADIUS, RADIUS + 1))[:, None] <= radius[None, :]).astype(jnp.float32)
    tempering = jnp.exp2(-temper.astype(jnp.float32))[:, None]
    indicator_floating = obs_mask.astype(jnp.float32)

    def rate_sample(sample_position):
        data_misfit = sample_position - measured_quantity
        loglik = -0.5 * indicator_floating * measured_confidence * data_misfit * data_misfit
        column_total = smooth(loglik, nearby_patch, -1)
        row_sum = smooth(column_total, nearby_patch, -2)
        return tempering * (row_sum[0] + row_sum[1] + row_sum[2])
    sample_fitness = lax.map(rate_sample, propagate_group)
    peak = lax.optimization_barrier(jnp.max(sample_fitness, axis=0))
    sample_importance = jnp.exp(sample_fitness - peak)
    sample_number = float(propagate_group.shape[0])
    total_weight = lax.optimization_barrier(jnp.sum(sample_importance, axis=0))
    updated_expectation = lax.optimization_barrier(jnp.sum(sample_importance[:, None] * propagate_group, axis=0))
    background_expectation = lax.optimization_barrier(jnp.sum(propagate_group, axis=0))
    updated_center = updated_expectation / total_weight
    background_center = background_expectation / sample_number
    quantity_tiles = propagate_group.reshape((N_MEMBER, ENSEMBLE_SLICE) + propagate_group.shape[1:])
    weight_blocks = sample_importance.reshape((N_MEMBER, ENSEMBLE_SLICE) + sample_importance.shape[1:])

    def accumulate(totals, block):
        fields, block_weights = block
        updated_spread = fields - updated_center
        background_spread = fields - background_center
        post_terms = jnp.stack([lax.optimization_barrier(jnp.sum(block_weights * updated_spread[:, couple[0]] * updated_spread[:, couple[1]], axis=0)) for couple in pair_list])
        prior_terms = jnp.stack([lax.optimization_barrier(jnp.sum(background_spread[:, couple[0]] * background_spread[:, couple[1]], axis=0)) for couple in pair_list])
        return ((totals[0] + post_terms, totals[1] + prior_terms), None)
    empty = jnp.zeros((6,) + total_weight.shape, jnp.float32)
    (post_second, prior_second), unused = lax.scan(accumulate, (empty, empty), (quantity_tiles, weight_blocks))
    post_cov = with_jitter(post_second, total_weight)
    prior_cov = with_jitter(prior_second, sample_number)
    neighbor_shifts, blend_matrix_lines = transform([updated_center[0], updated_center[1], updated_center[2]], post_cov, [background_center[0], background_center[1], background_center[2]], prior_cov)
    return correct_by_blend(propagate_group, neighbor_shifts, blend_matrix_lines)
```

```python
import jax
import jax.numpy as jnp
from jax import lax
from jax.experimental import pallas as pl
from jax.experimental.pallas import tpu as pltpu
from jax.sharding import Mesh, PartitionSpec as P

STEPS = 4
RADIUS = 4
LOCAL = 8
FIELDS = 3
X = 4
HALO = 8
STATS = 20
SLOT = 24
COEFS = 9
COEF_SLOT = 16

jitter = 0.05
pair_list = ((0, 0), (1, 0), (1, 1), (2, 0), (2, 1), (2, 2))
VMEM = pl.BlockSpec(memory_space=pltpu.VMEM)
SMEM = pl.BlockSpec(memory_space=pltpu.SMEM)


def cholesky_rows(matrix):
    first = jnp.sqrt(matrix[0])
    second = matrix[1] / first
    fourth = matrix[3] / first
    third = jnp.sqrt(matrix[2] - second * second)
    fifth = (matrix[4] - fourth * second) / third
    sixth = jnp.sqrt(matrix[5] - fourth * fourth - fifth * fifth)
    return [first, second, third, fourth, fifth, sixth]


def lower_inverse(packed):
    head = 1.0 / packed[0]
    middle = 1.0 / packed[2]
    tail = 1.0 / packed[5]
    below_head = -packed[1] * head * middle
    below_middle = -packed[4] * middle * tail
    corner = -(packed[3] * head + packed[4] * below_head) * tail
    return [head, below_head, middle, corner, below_middle, tail]


def lower_product(left_side, right_side):
    return [
        left_side[0] * right_side[0],
        left_side[1] * right_side[0] + left_side[2] * right_side[1],
        left_side[2] * right_side[2],
        left_side[3] * right_side[0] + left_side[4] * right_side[1] + left_side[5] * right_side[3],
        left_side[4] * right_side[2] + left_side[5] * right_side[4],
        left_side[5] * right_side[5],
    ]


def forecast_kernel(
    radius_ref, own_ref, above_ref, below_ref, own_par_ref, temper_ref,
    field_ref, stats_ref, par_ref, score_ref,
):
    rows = own_ref.shape[2]
    tall = rows + 2 * HALO

    def roll(value, shift, axis):
        return pltpu.roll(value, shift % value.shape[axis], axis)

    def bordered(plane):
        return jnp.concatenate(
            [above_ref[24 + plane], own_par_ref[plane], below_ref[24 + plane]], axis=0
        )

    spread, flow = bordered(0), bordered(1)
    par_ref[0] = 1.0 - 4.0 * spread - flow
    par_ref[1] = spread + flow
    par_ref[2] = spread
    for plane in range(6):
        par_ref[3 + plane] = bordered(2 + plane)

    weights = [
        [jnp.where(radius_ref[f] >= k, 1.0, 0.0) for k in range(1, RADIUS + 1)]
        for f in range(FIELDS)
    ]

    def one_member(m, carry):
        mixed = [None] * (RADIUS + 1)
        for f in range(FIELDS):
            plane = m * FIELDS + f
            value = jnp.concatenate(
                [above_ref[plane], own_ref[m, f], below_ref[plane]], axis=0
            )
            for _ in range(STEPS):
                above = roll(value, 1, 0)
                sides = roll(value, -1, 0) + roll(value, 1, 1) + roll(value, -1, 1)
                value = par_ref[0] * value + par_ref[1] * above + par_ref[2] * sides
            field_ref[m, f] = value[HALO : HALO + rows]
            misfit = value - par_ref[3 + f]
            loglik = par_ref[6 + f] * misfit * misfit
            total = loglik[HALO : HALO + rows]
            for k in range(1, RADIUS + 1):
                both = roll(loglik, k, 0) + roll(loglik, -k, 0)
                total = total + weights[f][k - 1] * both[HALO : HALO + rows]
            mixed[0] = total if f == 0 else mixed[0] + total
            for k in range(1, RADIUS + 1):
                term = weights[f][k - 1] * total
                mixed[k] = term if f == 0 else mixed[k] + term
        score = mixed[0]
        for k in range(1, RADIUS + 1):
            score = score + (roll(mixed[k], k, 1) + roll(mixed[k], -k, 1))
        score_ref[m] = temper_ref[...] * score
        return carry

    lax.fori_loop(0, LOCAL, one_member, 0)

    def one_group(g, carry):
        sub = pl.ds(pl.multiple_of(g * 8, 8), 8)
        for half in range(2):
            lane = pl.ds(half * 128, 128)
            scores = [score_ref[m, sub, lane] for m in range(LOCAL)]
            peak = scores[0]
            for m in range(1, LOCAL):
                peak = jnp.maximum(peak, scores[m])
            importance = [jnp.exp(s - peak) for s in scores]
            total = sum(importance[1:], importance[0])
            cells = [[field_ref[m, f, sub, lane] for f in range(FIELDS)] for m in range(LOCAL)]
            out = [peak, total]
            inverse = 1.0 / total
            for weighted in (True, False):
                means = []
                for f in range(FIELDS):
                    if weighted:
                        terms = [importance[m] * cells[m][f] for m in range(LOCAL)]
                        means.append(sum(terms[1:], terms[0]) * inverse)
                    else:
                        terms = [cells[m][f] for m in range(LOCAL)]
                        means.append(sum(terms[1:], terms[0]) * (1.0 / LOCAL))
                seconds = [None] * 6
                for m in range(LOCAL):
                    away = [cells[m][f] - means[f] for f in range(FIELDS)]
                    scaled = [importance[m] * a for a in away] if weighted else away
                    for number, (i, j) in enumerate(pair_list):
                        term = scaled[i] * away[j]
                        seconds[number] = term if m == 0 else seconds[number] + term
                out += means + seconds
            for number in range(STATS):
                stats_ref[g, number, :, lane] = out[number]
        return carry

    lax.fori_loop(0, rows // 8, one_group, 0)


def merged(parts, count, add, biggest):
    peak = biggest(parts[0])
    rescale = [jnp.exp(p - peak) for p in parts[0]]
    mass = [r * t for r, t in zip(rescale, parts[1])]
    total = add(mass)
    inverse = 1.0 / total
    sources = len(mass)
    out = [peak, total]
    means = [
        add([mass[s] * parts[2 + f][s] for s in range(sources)]) * inverse for f in range(FIELDS)
    ]
    away = [[parts[2 + f][s] - means[f] for s in range(sources)] for f in range(FIELDS)]
    out += means
    for number, (i, j) in enumerate(pair_list):
        out.append(
            add(
                [
                    rescale[s] * parts[5 + number][s] + mass[s] * away[i][s] * away[j][s]
                    for s in range(sources)
                ]
            )
        )
    n_sources, each = count
    means = [add(parts[11 + f]) * (1.0 / n_sources) for f in range(FIELDS)]
    away = [[parts[11 + f][s] - means[f] for s in range(sources)] for f in range(FIELDS)]
    out += means
    for number, (i, j) in enumerate(pair_list):
        out.append(
            add(
                [
                    parts[14 + number][s] + float(each) * (away[i][s] * away[j][s])
                    for s in range(sources)
                ]
            )
        )
    return out


def merge_x_kernel(part_ref, out_ref):
    def add(terms):
        return sum(terms[1:], terms[0])

    def biggest(terms):
        peak = terms[0]
        for t in terms[1:]:
            peak = jnp.maximum(peak, t)
        return peak

    for half in range(2):
        lane = pl.ds(half * 128, 128)
        parts = [[part_ref[s, p, :, lane] for s in range(X)] for p in range(STATS)]
        out = merged(parts, (X, LOCAL), add, biggest)
        for p in range(STATS):
            out_ref[pl.ds(half * 8 * SLOT + p, 8, stride=SLOT), :] = out[p]


def merge_z_kernel(part_ref, out_ref):
    sources = part_ref.shape[0] // SLOT
    blocks = sources // 8

    def add(terms):
        return jnp.sum(sum(terms[1:], terms[0]), axis=0, keepdims=True)

    def biggest(terms):
        peak = terms[0]
        for t in terms[1:]:
            peak = jnp.maximum(peak, t)
        return jnp.max(peak, axis=0, keepdims=True)

    parts = [
        [part_ref[pl.ds(b * 8 * SLOT + p, 8, stride=SLOT), :] for b in range(blocks)]
        for p in range(STATS)
    ]
    out = merged(parts, (sources, LOCAL * X), add, biggest)
    inverse = 1.0 / out[1]
    diagonal = (0, 2, 5)
    post_cov = [out[5 + n] * inverse + (jitter if n in diagonal else 0.0) for n in range(6)]
    scale = 1.0 / (sources * LOCAL * X)
    prior_cov = [out[14 + n] * scale + (jitter if n in diagonal else 0.0) for n in range(6)]
    gain = lower_product(cholesky_rows(post_cov), lower_inverse(cholesky_rows(prior_cov)))
    result = list(gain)
    for row in range(FIELDS):
        running = out[2 + row]
        for source in range(row + 1):
            running = running - gain[row * (row + 1) // 2 + source] * out[11 + source]
        result.append(running)
    for p in range(COEFS):
        value = jnp.broadcast_to(result[p], (8, 128))
        for b in range(blocks):
            out_ref[pl.ds(b * 8 * COEF_SLOT + p, 8, stride=COEF_SLOT), :] = value


def spread_kernel(coef_ref, out_ref):
    for half in range(2):
        lane = pl.ds(half * 128, 128)
        for p in range(COEFS):
            value = coef_ref[pl.ds(half * 8 * COEF_SLOT + p, 8, stride=COEF_SLOT), :]
            for target in range(X):
                out_ref[target, p, :, lane] = value


def apply_kernel(coef_ref, field_ref, out_ref):
    def one_group(g, carry):
        sub = pl.ds(pl.multiple_of(g * 8, 8), 8)
        coef = [coef_ref[g, p] for p in range(COEFS)]
        for m in range(LOCAL):
            cells = [field_ref[m, f, sub, :] for f in range(FIELDS)]
            for row in range(FIELDS):
                running = coef[6 + row]
                for source in range(row + 1):
                    running = running + coef[row * (row + 1) // 2 + source] * cells[source]
                out_ref[m, row, sub, :] = running
        return carry

    lax.fori_loop(0, X, one_group, 0)


def f32(*shape):
    return jax.ShapeDtypeStruct(shape, jnp.float32)


def body(
    sample_group,
    spreading_ratio,
    flow_ratio,
    measured_quantity,
    measured_confidence,
    obs_mask,
    radius,
    temper,
):
    rows, cols = sample_group.shape[2:]
    z = lax.axis_size("z")
    observed = -0.5 * obs_mask.astype(jnp.float32) * measured_confidence
    own_par = jnp.concatenate(
        [spreading_ratio[None], flow_ratio[None], measured_quantity, observed], axis=0
    )
    planes = sample_group.reshape(LOCAL * FIELDS, rows, cols)
    last = jnp.concatenate([planes[:, rows - HALO :], own_par[:, rows - HALO :]], axis=0)
    leading = jnp.concatenate([planes[:, :HALO], own_par[:, :HALO]], axis=0)
    count = lax.axis_size("space")
    up = [(i, (i + 1) % count) for i in range(count)]
    down = [(j, i) for i, j in up]
    above = lax.ppermute(last, "space", up)
    below = lax.ppermute(leading, "space", down)
    tempering = jnp.broadcast_to(jnp.exp2(-temper.astype(jnp.float32))[:, None], (rows, cols))

    field, stats = pl.pallas_call(
        forecast_kernel,
        out_shape=(f32(LOCAL, FIELDS, rows, cols), f32(X, STATS, 8, cols)),
        in_specs=[SMEM] + [VMEM] * 5,
        out_specs=(VMEM, VMEM),
        scratch_shapes=[
            pltpu.VMEM((9, rows + 2 * HALO, cols), jnp.float32),
            pltpu.VMEM((LOCAL, rows, cols), jnp.float32),
        ],
        name="forecast",
    )(radius, sample_group, above, below, own_par, tempering)

    stats = lax.all_to_all(stats, "x", 0, 0, tiled=True)
    stats = pl.pallas_call(
        merge_x_kernel,
        out_shape=f32(z * SLOT, 128),
        in_specs=[VMEM],
        out_specs=VMEM,
        name="merge_x",
    )(stats)
    stats = lax.all_to_all(stats.reshape(z, SLOT, 128), "z", 0, 0, tiled=True)
    coef = pl.pallas_call(
        merge_z_kernel,
        out_shape=f32(z * COEF_SLOT, 128),
        in_specs=[VMEM],
        out_specs=VMEM,
        name="merge_z",
    )(stats.reshape(z * SLOT, 128))
    coef = lax.all_to_all(coef.reshape(z, COEF_SLOT, 128), "z", 0, 0, tiled=True)
    coef = pl.pallas_call(
        spread_kernel,
        out_shape=f32(X, COEFS, 8, cols),
        in_specs=[VMEM],
        out_specs=VMEM,
        name="spread",
    )(coef.reshape(z * COEF_SLOT, 128))
    coef = lax.all_to_all(coef, "x", 0, 0, tiled=True)
    return pl.pallas_call(
        apply_kernel,
        out_shape=f32(LOCAL, FIELDS, rows, cols),
        in_specs=[VMEM, VMEM],
        out_specs=VMEM,
        name="apply",
    )(coef, field)


def solution(mesh):
    devices = mesh.devices
    fine = Mesh(devices.reshape(devices.shape[0] // X, X, devices.shape[1]), ("z", "x", "space"))
    member = ("z", "x")
    in_specs = (
        P(member, None, "space", None),
        P("space", None),
        P("space", None),
        P(None, "space", None),
        P(None, "space", None),
        P(None, "space", None),
        P(),
        P("space"),
    )
    out_specs = P(member, None, "space", None)
    return jax.shard_map(body, mesh=fine, in_specs=in_specs, out_specs=out_specs, check_vma=False)
```

```python
import jax
import jax.numpy as jnp
from jax import lax
from jax.experimental import pallas as pl
from jax.experimental.pallas import tpu as pltpu
from jax.sharding import Mesh, PartitionSpec as P

STEPS = 4
RADIUS = 4
LOCAL = 8
FIELDS = 3
X = 4
HALO = 8
STATS = 20
SLOT = 24
COEFS = 9
COEF_SLOT = 16

jitter = 0.05
pair_list = ((0, 0), (1, 0), (1, 1), (2, 0), (2, 1), (2, 2))
VMEM = pl.BlockSpec(memory_space=pltpu.VMEM)
SMEM = pl.BlockSpec(memory_space=pltpu.SMEM)

LARGE = pltpu.CompilerParams(vmem_limit_bytes=8 << 20)
SMALL = pltpu.CompilerParams(vmem_limit_bytes=2 << 20)


def cholesky_rows(matrix):
    first = jnp.sqrt(matrix[0])
    second = matrix[1] / first
    fourth = matrix[3] / first
    third = jnp.sqrt(matrix[2] - second * second)
    fifth = (matrix[4] - fourth * second) / third
    sixth = jnp.sqrt(matrix[5] - fourth * fourth - fifth * fifth)
    return [first, second, third, fourth, fifth, sixth]


def lower_inverse(packed):
    head = 1.0 / packed[0]
    middle = 1.0 / packed[2]
    tail = 1.0 / packed[5]
    below_head = -packed[1] * head * middle
    below_middle = -packed[4] * middle * tail
    corner = -(packed[3] * head + packed[4] * below_head) * tail
    return [head, below_head, middle, corner, below_middle, tail]


def lower_product(left_side, right_side):
    return [
        left_side[0] * right_side[0],
        left_side[1] * right_side[0] + left_side[2] * right_side[1],
        left_side[2] * right_side[2],
        left_side[3] * right_side[0] + left_side[4] * right_side[1] + left_side[5] * right_side[3],
        left_side[4] * right_side[2] + left_side[5] * right_side[4],
        left_side[5] * right_side[5],
    ]


def forecast_kernel(
    radius_ref, own_ref, above_ref, below_ref, own_par_ref, temper_ref,
    field_ref, stats_ref, par_ref, score_ref,
):
    rows = own_ref.shape[2]
    tall = rows + 2 * HALO

    def roll(value, shift, axis):
        return pltpu.roll(value, shift % value.shape[axis], axis)

    def bordered(plane):
        return jnp.concatenate(
            [above_ref[24 + plane], own_par_ref[plane], below_ref[24 + plane]], axis=0
        )

    spread, flow = bordered(0), bordered(1)
    par_ref[0] = 1.0 - 4.0 * spread - flow
    par_ref[1] = spread + flow
    par_ref[2] = spread
    for plane in range(6):
        par_ref[3 + plane] = bordered(2 + plane)

    weights = [
        [jnp.where(radius_ref[f] >= k, 1.0, 0.0) for k in range(1, RADIUS + 1)]
        for f in range(FIELDS)
    ]

    def one_member(m, carry):
        mixed = [None] * (RADIUS + 1)
        for f in range(FIELDS):
            plane = m * FIELDS + f
            value = jnp.concatenate(
                [above_ref[plane], own_ref[m, f], below_ref[plane]], axis=0
            )
            for _ in range(STEPS):
                above = roll(value, 1, 0)
                sides = roll(value, -1, 0) + roll(value, 1, 1) + roll(value, -1, 1)
                value = par_ref[0] * value + par_ref[1] * above + par_ref[2] * sides
            field_ref[m, f] = value[HALO : HALO + rows]
            misfit = value - par_ref[3 + f]
            loglik = par_ref[6 + f] * misfit * misfit
            total = loglik[HALO : HALO + rows]
            for k in range(1, RADIUS + 1):
                both = roll(loglik, k, 0) + roll(loglik, -k, 0)
                total = total + weights[f][k - 1] * both[HALO : HALO + rows]
            mixed[0] = total if f == 0 else mixed[0] + total
            for k in range(1, RADIUS + 1):
                term = weights[f][k - 1] * total
                mixed[k] = term if f == 0 else mixed[k] + term
        score = mixed[0]
        for k in range(1, RADIUS + 1):
            score = score + (roll(mixed[k], k, 1) + roll(mixed[k], -k, 1))
        score_ref[m] = temper_ref[...] * score
        return carry

    lax.fori_loop(0, LOCAL, one_member, 0)

    def one_group(g, carry):
        sub = pl.ds(pl.multiple_of(g * 8, 8), 8)
        for half in range(2):
            lane = pl.ds(half * 128, 128)
            scores = [score_ref[m, sub, lane] for m in range(LOCAL)]
            peak = scores[0]
            for m in range(1, LOCAL):
                peak = jnp.maximum(peak, scores[m])
            importance = [jnp.exp(s - peak) for s in scores]
            total = sum(importance[1:], importance[0])
            cells = [[field_ref[m, f, sub, lane] for f in range(FIELDS)] for m in range(LOCAL)]
            out = [peak, total]
            inverse = 1.0 / total
            for weighted in (True, False):
                means = []
                for f in range(FIELDS):
                    if weighted:
                        terms = [importance[m] * cells[m][f] for m in range(LOCAL)]
                        means.append(sum(terms[1:], terms[0]) * inverse)
                    else:
                        terms = [cells[m][f] for m in range(LOCAL)]
                        means.append(sum(terms[1:], terms[0]) * (1.0 / LOCAL))
                seconds = [None] * 6
                for m in range(LOCAL):
                    away = [cells[m][f] - means[f] for f in range(FIELDS)]
                    scaled = [importance[m] * a for a in away] if weighted else away
                    for number, (i, j) in enumerate(pair_list):
                        term = scaled[i] * away[j]
                        seconds[number] = term if m == 0 else seconds[number] + term
                out += means + seconds
            for number in range(STATS):
                stats_ref[g, number, :, lane] = out[number]
        return carry

    lax.fori_loop(0, rows // 8, one_group, 0)


def merged(parts, count, add, biggest):
    peak = biggest(parts[0])
    rescale = [jnp.exp(p - peak) for p in parts[0]]
    mass = [r * t for r, t in zip(rescale, parts[1])]
    total = add(mass)
    inverse = 1.0 / total
    sources = len(mass)
    out = [peak, total]
    means = [
        add([mass[s] * parts[2 + f][s] for s in range(sources)]) * inverse for f in range(FIELDS)
    ]
    away = [[parts[2 + f][s] - means[f] for s in range(sources)] for f in range(FIELDS)]
    out += means
    for number, (i, j) in enumerate(pair_list):
        out.append(
            add(
                [
                    rescale[s] * parts[5 + number][s] + mass[s] * away[i][s] * away[j][s]
                    for s in range(sources)
                ]
            )
        )
    n_sources, each = count
    means = [add(parts[11 + f]) * (1.0 / n_sources) for f in range(FIELDS)]
    away = [[parts[11 + f][s] - means[f] for s in range(sources)] for f in range(FIELDS)]
    out += means
    for number, (i, j) in enumerate(pair_list):
        out.append(
            add(
                [
                    parts[14 + number][s] + float(each) * (away[i][s] * away[j][s])
                    for s in range(sources)
                ]
            )
        )
    return out


def merge_x_kernel(part_ref, out_ref):
    def add(terms):
        return sum(terms[1:], terms[0])

    def biggest(terms):
        peak = terms[0]
        for t in terms[1:]:
            peak = jnp.maximum(peak, t)
        return peak

    for half in range(2):
        lane = pl.ds(half * 128, 128)
        parts = [[part_ref[s, p, :, lane] for s in range(X)] for p in range(STATS)]
        out = merged(parts, (X, LOCAL), add, biggest)
        for p in range(STATS):
            out_ref[pl.ds(half * 8 * SLOT + p, 8, stride=SLOT), :] = out[p]


def merge_z_kernel(part_ref, out_ref):
    sources = part_ref.shape[0] // SLOT
    blocks = sources // 8

    def add(terms):
        return jnp.sum(sum(terms[1:], terms[0]), axis=0, keepdims=True)

    def biggest(terms):
        peak = terms[0]
        for t in terms[1:]:
            peak = jnp.maximum(peak, t)
        return jnp.max(peak, axis=0, keepdims=True)

    parts = [
        [part_ref[pl.ds(b * 8 * SLOT + p, 8, stride=SLOT), :] for b in range(blocks)]
        for p in range(STATS)
    ]
    out = merged(parts, (sources, LOCAL * X), add, biggest)
    inverse = 1.0 / out[1]
    diagonal = (0, 2, 5)
    post_cov = [out[5 + n] * inverse + (jitter if n in diagonal else 0.0) for n in range(6)]
    scale = 1.0 / (sources * LOCAL * X)
    prior_cov = [out[14 + n] * scale + (jitter if n in diagonal else 0.0) for n in range(6)]
    gain = lower_product(cholesky_rows(post_cov), lower_inverse(cholesky_rows(prior_cov)))
    result = list(gain)
    for row in range(FIELDS):
        running = out[2 + row]
        for source in range(row + 1):
            running = running - gain[row * (row + 1) // 2 + source] * out[11 + source]
        result.append(running)
    for p in range(COEFS):
        value = jnp.broadcast_to(result[p], (8, 128))
        for b in range(blocks):
            out_ref[pl.ds(b * 8 * COEF_SLOT + p, 8, stride=COEF_SLOT), :] = value


def spread_kernel(coef_ref, out_ref):
    for half in range(2):
        lane = pl.ds(half * 128, 128)
        for p in range(COEFS):
            value = coef_ref[pl.ds(half * 8 * COEF_SLOT + p, 8, stride=COEF_SLOT), :]
            for target in range(X):
                out_ref[target, p, :, lane] = value


def apply_kernel(coef_ref, field_ref, out_ref):
    def one_group(g, carry):
        sub = pl.ds(pl.multiple_of(g * 8, 8), 8)
        coef = [coef_ref[g, p] for p in range(COEFS)]
        for m in range(LOCAL):
            cells = [field_ref[m, f, sub, :] for f in range(FIELDS)]
            for row in range(FIELDS):
                running = coef[6 + row]
                for source in range(row + 1):
                    running = running + coef[row * (row + 1) // 2 + source] * cells[source]
                out_ref[m, row, sub, :] = running
        return carry

    lax.fori_loop(0, X, one_group, 0)


def f32(*shape):
    return jax.ShapeDtypeStruct(shape, jnp.float32)


def body(
    sample_group,
    spreading_ratio,
    flow_ratio,
    measured_quantity,
    measured_confidence,
    obs_mask,
    radius,
    temper,
):
    rows, cols = sample_group.shape[2:]
    z = lax.axis_size("z")
    observed = -0.5 * obs_mask.astype(jnp.float32) * measured_confidence
    own_par = jnp.concatenate(
        [spreading_ratio[None], flow_ratio[None], measured_quantity, observed], axis=0
    )
    planes = sample_group.reshape(LOCAL * FIELDS, rows, cols)
    last = jnp.concatenate([planes[:, rows - HALO :], own_par[:, rows - HALO :]], axis=0)
    leading = jnp.concatenate([planes[:, :HALO], own_par[:, :HALO]], axis=0)
    count = lax.axis_size("space")
    up = [(i, (i + 1) % count) for i in range(count)]
    down = [(j, i) for i, j in up]
    above = lax.ppermute(last, "space", up)
    below = lax.ppermute(leading, "space", down)
    tempering = jnp.broadcast_to(jnp.exp2(-temper.astype(jnp.float32))[:, None], (rows, cols))

    field, stats = pl.pallas_call(
        forecast_kernel,
        out_shape=(f32(LOCAL, FIELDS, rows, cols), f32(X, STATS, 8, cols)),
        in_specs=[SMEM] + [VMEM] * 5,
        out_specs=(VMEM, VMEM),
        scratch_shapes=[
            pltpu.VMEM((9, rows + 2 * HALO, cols), jnp.float32),
            pltpu.VMEM((LOCAL, rows, cols), jnp.float32),
        ],
        compiler_params=LARGE,
        name="forecast",
    )(radius, sample_group, above, below, own_par, tempering)

    stats = lax.all_to_all(stats, "x", 0, 0, tiled=True)
    stats = pl.pallas_call(
        merge_x_kernel,
        out_shape=f32(z * SLOT, 128),
        in_specs=[VMEM],
        out_specs=VMEM,
        compiler_params=SMALL,
        name="merge_x",
    )(stats)
    stats = lax.all_to_all(stats.reshape(z, SLOT, 128), "z", 0, 0, tiled=True)
    coef = pl.pallas_call(
        merge_z_kernel,
        out_shape=f32(z * COEF_SLOT, 128),
        in_specs=[VMEM],
        out_specs=VMEM,
        compiler_params=SMALL,
        name="merge_z",
    )(stats.reshape(z * SLOT, 128))
    coef = lax.all_to_all(coef.reshape(z, COEF_SLOT, 128), "z", 0, 0, tiled=True)
    coef = pl.pallas_call(
        spread_kernel,
        out_shape=f32(X, COEFS, 8, cols),
        in_specs=[VMEM],
        out_specs=VMEM,
        compiler_params=SMALL,
        name="spread",
    )(coef.reshape(z * COEF_SLOT, 128))
    coef = lax.all_to_all(coef, "x", 0, 0, tiled=True)
    return pl.pallas_call(
        apply_kernel,
        out_shape=f32(LOCAL, FIELDS, rows, cols),
        in_specs=[VMEM, VMEM],
        out_specs=VMEM,
        compiler_params=LARGE,
        name="apply",
    )(coef, field)


def solution(mesh):
    devices = mesh.devices
    fine = Mesh(devices.reshape(devices.shape[0] // X, X, devices.shape[1]), ("z", "x", "space"))
    member = ("z", "x")
    in_specs = (
        P(member, None, "space", None),
        P("space", None),
        P("space", None),
        P(None, "space", None),
        P(None, "space", None),
        P(None, "space", None),
        P(),
        P("space"),
    )
    out_specs = P(member, None, "space", None)
    return jax.shard_map(body, mesh=fine, in_specs=in_specs, out_specs=out_specs, check_vma=False)
```

```python
import jax
import jax.numpy as jnp
from jax import lax
from jax.experimental import pallas as pl
from jax.experimental.pallas import tpu as pltpu
from jax.sharding import Mesh, PartitionSpec as P

STEPS = 4
RADIUS = 4
LOCAL = 8
FIELDS = 3
X = 4
HALO = 8
STATS = 19
COEFS = 9

jitter = 0.05
pair_list = ((0, 0), (1, 0), (1, 1), (2, 0), (2, 1), (2, 2))
VMEM = pl.BlockSpec(memory_space=pltpu.VMEM)
SMEM = pl.BlockSpec(memory_space=pltpu.SMEM)

LARGE = pltpu.CompilerParams(vmem_limit_bytes=8 << 20)
SMALL = pltpu.CompilerParams(vmem_limit_bytes=2 << 20)


def cholesky_rows(matrix):
    first = jnp.sqrt(matrix[0])
    second = matrix[1] / first
    fourth = matrix[3] / first
    third = jnp.sqrt(matrix[2] - second * second)
    fifth = (matrix[4] - fourth * second) / third
    sixth = jnp.sqrt(matrix[5] - fourth * fourth - fifth * fifth)
    return [first, second, third, fourth, fifth, sixth]


def lower_inverse(packed):
    head = 1.0 / packed[0]
    middle = 1.0 / packed[2]
    tail = 1.0 / packed[5]
    below_head = -packed[1] * head * middle
    below_middle = -packed[4] * middle * tail
    corner = -(packed[3] * head + packed[4] * below_head) * tail
    return [head, below_head, middle, corner, below_middle, tail]


def lower_product(left_side, right_side):
    return [
        left_side[0] * right_side[0],
        left_side[1] * right_side[0] + left_side[2] * right_side[1],
        left_side[2] * right_side[2],
        left_side[3] * right_side[0] + left_side[4] * right_side[1] + left_side[5] * right_side[3],
        left_side[4] * right_side[2] + left_side[5] * right_side[4],
        left_side[5] * right_side[5],
    ]


def forecast_kernel(
    radius_ref, own_ref, above_ref, below_ref, own_par_ref, temper_ref,
    field_ref, stats_ref, par_ref, score_ref,
):
    rows = own_ref.shape[2]
    tall = rows + 2 * HALO

    def roll(value, shift, axis):
        return pltpu.roll(value, shift % value.shape[axis], axis)

    def bordered(plane):
        return jnp.concatenate(
            [above_ref[24 + plane], own_par_ref[plane], below_ref[24 + plane]], axis=0
        )

    spread, flow = bordered(0), bordered(1)
    par_ref[0] = 1.0 - 4.0 * spread - flow
    par_ref[1] = spread + flow
    par_ref[2] = spread
    for plane in range(6):
        par_ref[3 + plane] = bordered(2 + plane)

    weights = [
        [jnp.where(radius_ref[f] >= k, 1.0, 0.0) for k in range(1, RADIUS + 1)]
        for f in range(FIELDS)
    ]

    def one_member(m, carry):
        mixed = [None] * (RADIUS + 1)
        for f in range(FIELDS):
            plane = m * FIELDS + f
            value = jnp.concatenate(
                [above_ref[plane], own_ref[m, f], below_ref[plane]], axis=0
            )
            for _ in range(STEPS):
                above = roll(value, 1, 0)
                sides = roll(value, -1, 0) + roll(value, 1, 1) + roll(value, -1, 1)
                value = par_ref[0] * value + par_ref[1] * above + par_ref[2] * sides
            field_ref[m, f] = value[HALO : HALO + rows]
            misfit = value - par_ref[3 + f]
            loglik = par_ref[6 + f] * misfit * misfit
            total = loglik[HALO : HALO + rows]
            for k in range(1, RADIUS + 1):
                both = roll(loglik, k, 0) + roll(loglik, -k, 0)
                total = total + weights[f][k - 1] * both[HALO : HALO + rows]
            mixed[0] = total if f == 0 else mixed[0] + total
            for k in range(1, RADIUS + 1):
                term = weights[f][k - 1] * total
                mixed[k] = term if f == 0 else mixed[k] + term
        score = mixed[0]
        for k in range(1, RADIUS + 1):
            score = score + (roll(mixed[k], k, 1) + roll(mixed[k], -k, 1))
        score_ref[m] = temper_ref[...] * score
        return carry

    lax.fori_loop(0, LOCAL, one_member, 0)

    def one_group(g, carry):
        sub = pl.ds(pl.multiple_of(g * 8, 8), 8)
        for half in range(2):
            lane = pl.ds(half * 128, 128)
            scores = [score_ref[m, sub, lane] for m in range(LOCAL)]
            peak = scores[0]
            for m in range(1, LOCAL):
                peak = jnp.maximum(peak, scores[m])
            importance = [jnp.exp(s - peak) for s in scores]
            total = sum(importance[1:], importance[0])
            cells = [[field_ref[m, f, sub, lane] for f in range(FIELDS)] for m in range(LOCAL)]
            out = [peak + jnp.log(total)]
            inverse = 1.0 / total
            for weighted in (True, False):
                means = []
                for f in range(FIELDS):
                    if weighted:
                        terms = [importance[m] * cells[m][f] for m in range(LOCAL)]
                        means.append(sum(terms[1:], terms[0]) * inverse)
                    else:
                        terms = [cells[m][f] for m in range(LOCAL)]
                        means.append(sum(terms[1:], terms[0]) * (1.0 / LOCAL))
                seconds = [None] * 6
                for m in range(LOCAL):
                    away = [cells[m][f] - means[f] for f in range(FIELDS)]
                    scaled = [importance[m] * a for a in away] if weighted else away
                    for number, (i, j) in enumerate(pair_list):
                        term = scaled[i] * away[j]
                        seconds[number] = term if m == 0 else seconds[number] + term
                share = inverse if weighted else 1.0 / LOCAL
                out += means + [share * second for second in seconds]
            for number in range(STATS):
                stats_ref[g, number, :, lane] = out[number]
        return carry

    lax.fori_loop(0, rows // 8, one_group, 0)


def merged(parts, add, biggest):
    peak = biggest(parts[0])
    mass = [jnp.exp(p - peak) for p in parts[0]]
    total = add(mass)
    out = [peak + jnp.log(total)]
    for first, weights in ((1, mass), (10, None)):
        count = len(mass)

        def average(terms):
            if weights is None:
                return add(terms)
            return add([weights[s] * terms[s] for s in range(count)])

        share = 1.0 / (total if weights is not None else add([jnp.ones_like(m) for m in mass]))
        means = [average(parts[first + f]) * share for f in range(FIELDS)]
        away = [[parts[first + f][s] - means[f] for s in range(count)] for f in range(FIELDS)]
        out += means
        for number, (i, j) in enumerate(pair_list):
            second = parts[first + FIELDS + number]
            out.append(
                average([second[s] + away[i][s] * away[j][s] for s in range(count)]) * share
            )
    return out


def merge_x_kernel(part_ref, out_ref):
    def add(terms):
        return sum(terms[1:], terms[0])

    def biggest(terms):
        peak = terms[0]
        for t in terms[1:]:
            peak = jnp.maximum(peak, t)
        return peak

    for half in range(2):
        lane = pl.ds(half * 128, 128)
        parts = [[part_ref[s, p, :, lane] for s in range(X)] for p in range(STATS)]
        out = merged(parts, add, biggest)
        for p in range(STATS):
            out_ref[pl.ds(half * 8 * STATS + p, 8, stride=STATS), :] = out[p]


def merge_z_kernel(part_ref, out_ref):
    sources = part_ref.shape[0] // STATS
    blocks = sources // 8

    def add(terms):
        return jnp.sum(sum(terms[1:], terms[0]), axis=0, keepdims=True)

    def biggest(terms):
        peak = terms[0]
        for t in terms[1:]:
            peak = jnp.maximum(peak, t)
        return jnp.max(peak, axis=0, keepdims=True)

    parts = [
        [part_ref[pl.ds(b * 8 * STATS + p, 8, stride=STATS), :] for b in range(blocks)]
        for p in range(STATS)
    ]
    out = merged(parts, add, biggest)
    diagonal = (0, 2, 5)
    post_cov = [out[4 + n] + (jitter if n in diagonal else 0.0) for n in range(6)]
    prior_cov = [out[13 + n] + (jitter if n in diagonal else 0.0) for n in range(6)]
    gain = lower_product(cholesky_rows(post_cov), lower_inverse(cholesky_rows(prior_cov)))
    result = list(gain)
    for row in range(FIELDS):
        running = out[1 + row]
        for source in range(row + 1):
            running = running - gain[row * (row + 1) // 2 + source] * out[10 + source]
        result.append(running)
    for p in range(COEFS):
        value = jnp.broadcast_to(result[p], (8, 128))
        for b in range(blocks):
            out_ref[pl.ds(b * 8 * COEFS + p, 8, stride=COEFS), :] = value


def spread_kernel(coef_ref, out_ref):
    for half in range(2):
        lane = pl.ds(half * 128, 128)
        for p in range(COEFS):
            value = coef_ref[pl.ds(half * 8 * COEFS + p, 8, stride=COEFS), :]
            for target in range(X):
                out_ref[target, p, :, lane] = value


def apply_kernel(coef_ref, field_ref, out_ref):
    def one_group(g, carry):
        sub = pl.ds(pl.multiple_of(g * 8, 8), 8)
        coef = [coef_ref[g, p] for p in range(COEFS)]
        for m in range(LOCAL):
            cells = [field_ref[m, f, sub, :] for f in range(FIELDS)]
            for row in range(FIELDS):
                running = coef[6 + row]
                for source in range(row + 1):
                    running = running + coef[row * (row + 1) // 2 + source] * cells[source]
                out_ref[m, row, sub, :] = running
        return carry

    lax.fori_loop(0, X, one_group, 0)


def f32(*shape):
    return jax.ShapeDtypeStruct(shape, jnp.float32)


def body(
    sample_group,
    spreading_ratio,
    flow_ratio,
    measured_quantity,
    measured_confidence,
    obs_mask,
    radius,
    temper,
):
    rows, cols = sample_group.shape[2:]
    z = lax.axis_size("z")
    observed = -0.5 * obs_mask.astype(jnp.float32) * measured_confidence
    own_par = jnp.concatenate(
        [spreading_ratio[None], flow_ratio[None], measured_quantity, observed], axis=0
    )
    planes = sample_group.reshape(LOCAL * FIELDS, rows, cols)
    last = jnp.concatenate([planes[:, rows - HALO :], own_par[:, rows - HALO :]], axis=0)
    leading = jnp.concatenate([planes[:, :HALO], own_par[:, :HALO]], axis=0)
    count = lax.axis_size("space")
    up = [(i, (i + 1) % count) for i in range(count)]
    down = [(j, i) for i, j in up]
    above = lax.ppermute(last, "space", up)
    below = lax.ppermute(leading, "space", down)
    tempering = jnp.broadcast_to(jnp.exp2(-temper.astype(jnp.float32))[:, None], (rows, cols))

    field, stats = pl.pallas_call(
        forecast_kernel,
        out_shape=(f32(LOCAL, FIELDS, rows, cols), f32(X, STATS, 8, cols)),
        in_specs=[SMEM] + [VMEM] * 5,
        out_specs=(VMEM, VMEM),
        scratch_shapes=[
            pltpu.VMEM((9, rows + 2 * HALO, cols), jnp.float32),
            pltpu.VMEM((LOCAL, rows, cols), jnp.float32),
        ],
        compiler_params=LARGE,
        name="forecast",
    )(radius, sample_group, above, below, own_par, tempering)

    stats = lax.all_to_all(stats, "x", 0, 0, tiled=True)
    stats = pl.pallas_call(
        merge_x_kernel,
        out_shape=f32(z * STATS, 128),
        in_specs=[VMEM],
        out_specs=VMEM,
        compiler_params=SMALL,
        name="merge_x",
    )(stats)
    stats = lax.all_to_all(stats.reshape(z, STATS, 1, 128), "z", 0, 0, tiled=True)
    coef = pl.pallas_call(
        merge_z_kernel,
        out_shape=f32(z * COEFS, 128),
        in_specs=[VMEM],
        out_specs=VMEM,
        compiler_params=SMALL,
        name="merge_z",
    )(stats.reshape(z * STATS, 128))
    coef = lax.all_to_all(coef.reshape(z, COEFS, 1, 128), "z", 0, 0, tiled=True)
    coef = pl.pallas_call(
        spread_kernel,
        out_shape=f32(X, COEFS, 8, cols),
        in_specs=[VMEM],
        out_specs=VMEM,
        compiler_params=SMALL,
        name="spread",
    )(coef.reshape(z * COEFS, 128))
    coef = lax.all_to_all(coef, "x", 0, 0, tiled=True)
    return pl.pallas_call(
        apply_kernel,
        out_shape=f32(LOCAL, FIELDS, rows, cols),
        in_specs=[VMEM, VMEM],
        out_specs=VMEM,
        compiler_params=LARGE,
        name="apply",
    )(coef, field)


def solution(mesh):
    devices = mesh.devices
    fine = Mesh(devices.reshape(devices.shape[0] // X, X, devices.shape[1]), ("z", "x", "space"))
    member = ("z", "x")
    in_specs = (
        P(member, None, "space", None),
        P("space", None),
        P("space", None),
        P(None, "space", None),
        P(None, "space", None),
        P(None, "space", None),
        P(),
        P("space"),
    )
    out_specs = P(member, None, "space", None)
    return jax.shard_map(body, mesh=fine, in_specs=in_specs, out_specs=out_specs, check_vma=False)
```

```python
import jax
import jax.numpy as jnp
from jax import lax
from jax.experimental import pallas as pl
from jax.experimental.pallas import tpu as pltpu
from jax.sharding import Mesh, PartitionSpec as P

STEPS = 4
RADIUS = 4
LOCAL = 8
FIELDS = 3
X = 4
HALO = 8
STATS = 19
COEFS = 9

jitter = 0.05
pair_list = ((0, 0), (1, 0), (1, 1), (2, 0), (2, 1), (2, 2))
VMEM = pl.BlockSpec(memory_space=pltpu.VMEM)
SMEM = pl.BlockSpec(memory_space=pltpu.SMEM)

LARGE = pltpu.CompilerParams(vmem_limit_bytes=8 << 20)
SMALL = pltpu.CompilerParams(vmem_limit_bytes=2 << 20)


def cholesky_rows(matrix):
    first = jnp.sqrt(matrix[0])
    second = matrix[1] / first
    fourth = matrix[3] / first
    third = jnp.sqrt(matrix[2] - second * second)
    fifth = (matrix[4] - fourth * second) / third
    sixth = jnp.sqrt(matrix[5] - fourth * fourth - fifth * fifth)
    return [first, second, third, fourth, fifth, sixth]


def lower_inverse(packed):
    head = 1.0 / packed[0]
    middle = 1.0 / packed[2]
    tail = 1.0 / packed[5]
    below_head = -packed[1] * head * middle
    below_middle = -packed[4] * middle * tail
    corner = -(packed[3] * head + packed[4] * below_head) * tail
    return [head, below_head, middle, corner, below_middle, tail]


def lower_product(left_side, right_side):
    return [
        left_side[0] * right_side[0],
        left_side[1] * right_side[0] + left_side[2] * right_side[1],
        left_side[2] * right_side[2],
        left_side[3] * right_side[0] + left_side[4] * right_side[1] + left_side[5] * right_side[3],
        left_side[4] * right_side[2] + left_side[5] * right_side[4],
        left_side[5] * right_side[5],
    ]


HALF = 128
PAD = 8


def split(value):
    return value[:, :HALF], value[:, HALF:]


def lane_sides(pair, k):
    a, b = pair
    lane = lax.broadcasted_iota(jnp.int32, a.shape, 1)
    low, high = lane < k, lane >= HALF - k
    left_a, left_b = pltpu.roll(a, k, 1), pltpu.roll(b, k, 1)
    right_a, right_b = pltpu.roll(a, HALF - k, 1), pltpu.roll(b, HALF - k, 1)
    return (
        jnp.where(low, left_b, left_a) + jnp.where(high, right_b, right_a),
        jnp.where(low, left_a, left_b) + jnp.where(high, right_a, right_b),
    )


def advance(pair, buffer_ref, coef_ref):
    rows = pair[0].shape[0]
    for step in range(STEPS):
        slot = buffer_ref.at[step % 2]
        for h in range(2):
            slot[h, PAD : PAD + rows] = pair[h]
        sides = lane_sides(pair, 1)
        pair = tuple(
            coef_ref[0, h] * pair[h]
            + coef_ref[1, h] * slot[h, PAD - 1 : PAD - 1 + rows]
            + coef_ref[2, h] * (slot[h, PAD + 1 : PAD + 1 + rows] + sides[h])
            for h in range(2)
        )
    return pair


def radius_weights(radius_ref):
    return [
        [None, None] + [jnp.where(radius_ref[f] >= k, 1.0, 0.0) for k in range(2, RADIUS + 1)]
        for f in range(FIELDS)
    ]


def row_total(likelihood_ref, start, rows, weights):
    def both(k):
        return (
            likelihood_ref[start - k : start - k + rows]
            + likelihood_ref[start + k : start + k + rows]
        )

    outer = both(RADIUS)
    for k in range(RADIUS - 1, 0, -1):
        outer = both(k) + weights[k + 1] * outer
    return likelihood_ref[start : start + rows] + outer


def column_total(totals, weights):
    score = tuple(sum((t[h] for t in totals[1:]), totals[0][h]) for h in range(2))
    mixed = score
    for k in range(1, RADIUS + 1):
        if k > 1:
            totals = [
                tuple(weights[f][k] * t for t in totals[f]) for f in range(FIELDS)
            ]
            mixed = tuple(sum((t[h] for t in totals[1:]), totals[0][h]) for h in range(2))
        sides = lane_sides(mixed, k)
        score = tuple(score[h] + sides[h] for h in range(2))
    return score


def local_statistics(scores, cells):
    def plus(terms):
        return sum(terms[1:], terms[0])

    peak = scores[0]
    for s in scores[1:]:
        peak = jnp.maximum(peak, s)
    importance = [jnp.exp(s - peak) for s in scores]
    total = plus(importance)
    inverse = 1.0 / total
    share = 1.0 / LOCAL
    center = [plus([c[f] for c in cells]) * share for f in range(FIELDS)]
    away = [[c[f] - center[f] for f in range(FIELDS)] for c in cells]
    drift = [
        plus([w * a[f] for w, a in zip(importance, away)]) * inverse for f in range(FIELDS)
    ]
    post, prior = [], []
    for i, j in pair_list:
        products = [a[i] * a[j] for a in away]
        prior.append(plus(products) * share)
        post.append(
            plus([w * p for w, p in zip(importance, products)]) * inverse - drift[i] * drift[j]
        )
    moved = [center[f] + drift[f] for f in range(FIELDS)]
    return [peak + jnp.log(total)] + moved + post + center + prior


def interior_kernel(
    radius_ref, own_ref, par_ref, temper_ref, field_ref, stats_ref,
    coef_ref, buffer_ref, likelihood_ref, score_ref,
):
    rows = own_ref.shape[2]
    inner = rows - 16
    spread, flow = split(par_ref[0]), split(par_ref[1])
    for h in range(2):
        coef_ref[0, h] = 1.0 - 4.0 * spread[h] - flow[h]
        coef_ref[1, h] = spread[h] + flow[h]
        coef_ref[2, h] = spread[h]
    weights = radius_weights(radius_ref)

    def one_member(m, carry):
        totals = []
        for f in range(FIELDS):
            pair = advance(split(own_ref[m, f]), buffer_ref.at[f], coef_ref)
            quantity, observed = split(par_ref[2 + f]), split(par_ref[5 + f])
            for h in range(2):
                field_ref[m, f, h] = pair[h]
                misfit = pair[h] - quantity[h]
                likelihood_ref[f, h] = observed[h] * misfit * misfit
            totals.append(
                tuple(row_total(likelihood_ref.at[f, h], 8, inner, weights[f]) for h in range(2))
            )
        score = column_total(totals, weights)
        for h in range(2):
            score_ref[m, h] = temper_ref[8 : 8 + inner] * score[h]
        return carry

    lax.fori_loop(0, LOCAL, one_member, 0)

    def one_group(g, carry):
        sub = pl.ds(pl.multiple_of(g * 8, 8), 8)
        deep = pl.ds(pl.multiple_of(g * 8 + 8, 8), 8)
        for h in range(2):
            scores = [score_ref[m, h, sub] for m in range(LOCAL)]
            cells = [[field_ref[m, f, h, deep] for f in range(FIELDS)] for m in range(LOCAL)]
            for number, value in enumerate(local_statistics(scores, cells)):
                stats_ref[g, number, :, h * HALF : (h + 1) * HALF] = value
        return carry

    lax.fori_loop(0, inner // 8, one_group, 0)


def edge_kernel(
    radius_ref, own_ref, above_ref, below_ref, own_par_ref, temper_ref, inner_field_ref,
    inner_stats_ref, field_ref, stats_ref, coef_ref, buffer_ref, par_ref, wide_ref,
    likelihood_ref, score_ref,
):
    rows = own_ref.shape[2]
    ends = (slice(0, 8), slice(rows - 8, rows))
    base = FIELDS * LOCAL
    for g in range(rows // 8 - 2):
        stats_ref[1 + g] = inner_stats_ref[g]

    def framed(end, own, halo):
        return jnp.concatenate([halo, own] if end == 0 else [own, halo], axis=0)

    for end in range(2):
        halo_ref = (above_ref, below_ref)[end]
        spread = split(framed(end, own_par_ref[0, ends[end]], halo_ref[base]))
        flow = split(framed(end, own_par_ref[1, ends[end]], halo_ref[base + 1]))
        for h in range(2):
            coef_ref[end, 0, h] = 1.0 - 4.0 * spread[h] - flow[h]
            coef_ref[end, 1, h] = spread[h] + flow[h]
            coef_ref[end, 2, h] = spread[h]
    for p in range(6):
        for h in range(2):
            lane = slice(h * HALF, (h + 1) * HALF)
            par_ref[p, h, 0:8] = above_ref[base + 2 + p, :, lane]
            par_ref[p, h, 8 : 8 + rows] = own_par_ref[2 + p, :, lane]
            par_ref[p, h, 8 + rows : 16 + rows] = below_ref[base + 2 + p, :, lane]
    weights = radius_weights(radius_ref)

    def one_member(m, carry):
        for end in range(2):
            halo_ref = (above_ref, below_ref)[end]
            first = (4, rows - 4)[end]
            totals = []
            for f in range(FIELDS):
                start = framed(end, own_ref[m, f, ends[end]], halo_ref[m * FIELDS + f])
                pair = advance(split(start), buffer_ref.at[end, f], coef_ref.at[end])
                total = []
                for h in range(2):
                    wide = wide_ref.at[end, f, h]
                    fresh = buffer_ref.at[end, f, 0, h]
                    fresh[PAD : PAD + 16] = pair[h]
                    new = fresh[PAD + 4 : PAD + 12]
                    old = inner_field_ref[m, f, h, (4, rows - 12)[end] : (12, rows - 4)[end]]
                    wide[0:8] = (new, old)[end]
                    wide[8:16] = (old, new)[end]
                    field_ref[m, f, end, h] = wide[4:12]
                    misfit = framed(end, old, new) - par_ref[f, h, first : first + 16]
                    like = likelihood_ref.at[end, f, h]
                    like[...] = par_ref[3 + f, h, first : first + 16] * misfit * misfit
                    total.append(row_total(like, 4, 8, weights[f]))
                totals.append(tuple(total))
            score = column_total(totals, weights)
            for h in range(2):
                score_ref[m, end, h] = temper_ref[ends[end]] * score[h]
        return carry

    lax.fori_loop(0, LOCAL, one_member, 0)

    def one_half(h, carry):
        lane = pl.ds(pl.multiple_of(h * HALF, HALF), HALF)
        for end in range(2):
            scores = [score_ref[m, end, h] for m in range(LOCAL)]
            cells = [[field_ref[m, f, end, h] for f in range(FIELDS)] for m in range(LOCAL)]
            for number, value in enumerate(local_statistics(scores, cells)):
                stats_ref[(0, rows // 8 - 1)[end], number, :, lane] = value
        return carry

    lax.fori_loop(0, 2, one_half, 0)


def merged(parts, add, biggest):
    peak = biggest(parts[0])
    mass = [jnp.exp(p - peak) for p in parts[0]]
    total = add(mass)
    out = [peak + jnp.log(total)]
    for first, weights in ((1, mass), (10, None)):
        count = len(mass)

        def average(terms):
            if weights is None:
                return add(terms)
            return add([weights[s] * terms[s] for s in range(count)])

        share = 1.0 / (total if weights is not None else add([jnp.ones_like(m) for m in mass]))
        means = [average(parts[first + f]) * share for f in range(FIELDS)]
        away = [[parts[first + f][s] - means[f] for s in range(count)] for f in range(FIELDS)]
        out += means
        for number, (i, j) in enumerate(pair_list):
            second = parts[first + FIELDS + number]
            out.append(
                average([second[s] + away[i][s] * away[j][s] for s in range(count)]) * share
            )
    return out


def merge_x_kernel(part_ref, out_ref):
    def add(terms):
        return sum(terms[1:], terms[0])

    def biggest(terms):
        peak = terms[0]
        for t in terms[1:]:
            peak = jnp.maximum(peak, t)
        return peak

    for half in range(2):
        lane = pl.ds(half * 128, 128)
        parts = [[part_ref[s, p, :, lane] for s in range(X)] for p in range(STATS)]
        out = merged(parts, add, biggest)
        for p in range(STATS):
            out_ref[pl.ds(half * 8 * STATS + p, 8, stride=STATS), :] = out[p]


def merge_z_kernel(part_ref, out_ref):
    sources = part_ref.shape[0] // STATS
    blocks = sources // 8

    def add(terms):
        return jnp.sum(sum(terms[1:], terms[0]), axis=0, keepdims=True)

    def biggest(terms):
        peak = terms[0]
        for t in terms[1:]:
            peak = jnp.maximum(peak, t)
        return jnp.max(peak, axis=0, keepdims=True)

    parts = [
        [part_ref[pl.ds(b * 8 * STATS + p, 8, stride=STATS), :] for b in range(blocks)]
        for p in range(STATS)
    ]
    out = merged(parts, add, biggest)
    diagonal = (0, 2, 5)
    post_cov = [out[4 + n] + (jitter if n in diagonal else 0.0) for n in range(6)]
    prior_cov = [out[13 + n] + (jitter if n in diagonal else 0.0) for n in range(6)]
    gain = lower_product(cholesky_rows(post_cov), lower_inverse(cholesky_rows(prior_cov)))
    result = list(gain)
    for row in range(FIELDS):
        running = out[1 + row]
        for source in range(row + 1):
            running = running - gain[row * (row + 1) // 2 + source] * out[10 + source]
        result.append(running)
    for p in range(COEFS):
        value = jnp.broadcast_to(result[p], (8, 128))
        for b in range(blocks):
            out_ref[pl.ds(b * 8 * COEFS + p, 8, stride=COEFS), :] = value


def spread_kernel(coef_ref, out_ref):
    for half in range(2):
        lane = pl.ds(half * 128, 128)
        for p in range(COEFS):
            value = coef_ref[pl.ds(half * 8 * COEFS + p, 8, stride=COEFS), :]
            for target in range(X):
                out_ref[target, p, :, lane] = value


def apply_kernel(coef_ref, inner_ref, edge_ref, out_ref):
    last = X - 1

    def one_member(m, carry):
        for g in range(X):
            for h in range(2):
                lane = slice(h * HALF, (h + 1) * HALF)
                if g in (0, last):
                    cells = [edge_ref[m, f, 0 if g == 0 else 1, h] for f in range(FIELDS)]
                else:
                    cells = [inner_ref[m, f, h, g * 8 : g * 8 + 8] for f in range(FIELDS)]
                for row in range(FIELDS):
                    running = coef_ref[g, 6 + row, :, lane]
                    for source in range(row + 1):
                        entry = coef_ref[g, row * (row + 1) // 2 + source, :, lane]
                        running = running + entry * cells[source]
                    out_ref[m, row, g * 8 : g * 8 + 8, lane] = running
        return carry

    lax.fori_loop(0, LOCAL, one_member, 0)


def f32(*shape):
    return jax.ShapeDtypeStruct(shape, jnp.float32)


def body(
    sample_group,
    spreading_ratio,
    flow_ratio,
    measured_quantity,
    measured_confidence,
    obs_mask,
    radius,
    temper,
):
    rows, cols = sample_group.shape[2:]
    z = lax.axis_size("z")
    observed = -0.5 * obs_mask.astype(jnp.float32) * measured_confidence
    own_par = jnp.concatenate(
        [spreading_ratio[None], flow_ratio[None], measured_quantity, observed], axis=0
    )
    planes = sample_group.reshape(LOCAL * FIELDS, rows, cols)
    last = jnp.concatenate([planes[:, rows - HALO :], own_par[:, rows - HALO :]], axis=0)
    leading = jnp.concatenate([planes[:, :HALO], own_par[:, :HALO]], axis=0)
    count = lax.axis_size("space")
    up = [(i, (i + 1) % count) for i in range(count)]
    down = [(j, i) for i, j in up]
    above = lax.ppermute(last, "space", up)
    below = lax.ppermute(leading, "space", down)
    tempering = jnp.broadcast_to(jnp.exp2(-temper.astype(jnp.float32))[:, None], (rows, HALF))

    inner_field, inner_stats = pl.pallas_call(
        interior_kernel,
        out_shape=(f32(LOCAL, FIELDS, 2, rows, HALF), f32(rows // 8 - 2, STATS, 8, cols)),
        in_specs=[SMEM] + [VMEM] * 3,
        out_specs=(VMEM, VMEM),
        scratch_shapes=[
            pltpu.VMEM((3, 2, rows, HALF), jnp.float32),
            pltpu.VMEM((FIELDS, 2, 2, rows + 2 * PAD, HALF), jnp.float32),
            pltpu.VMEM((FIELDS, 2, rows, HALF), jnp.float32),
            pltpu.VMEM((LOCAL, 2, rows - 16, HALF), jnp.float32),
        ],
        compiler_params=LARGE,
        name="interior",
    )(radius, sample_group, own_par, tempering)

    edge_field, stats = pl.pallas_call(
        edge_kernel,
        out_shape=(f32(LOCAL, FIELDS, 2, 2, 8, HALF), f32(X, STATS, 8, cols)),
        in_specs=[SMEM] + [VMEM] * 7,
        out_specs=(VMEM, VMEM),
        scratch_shapes=[
            pltpu.VMEM((2, 3, 2, 16, HALF), jnp.float32),
            pltpu.VMEM((2, FIELDS, 2, 2, 16 + 2 * PAD, HALF), jnp.float32),
            pltpu.VMEM((6, 2, rows + 16, HALF), jnp.float32),
            pltpu.VMEM((2, FIELDS, 2, 16, HALF), jnp.float32),
            pltpu.VMEM((2, FIELDS, 2, 16, HALF), jnp.float32),
            pltpu.VMEM((LOCAL, 2, 2, 8, HALF), jnp.float32),
        ],
        compiler_params=LARGE,
        name="edge",
    )(radius, sample_group, above, below, own_par, tempering, inner_field, inner_stats)

    stats = lax.all_to_all(stats, "x", 0, 0, tiled=True)
    stats = pl.pallas_call(
        merge_x_kernel,
        out_shape=f32(z * STATS, 128),
        in_specs=[VMEM],
        out_specs=VMEM,
        compiler_params=SMALL,
        name="merge_x",
    )(stats)
    stats = lax.all_to_all(stats.reshape(z, STATS, 1, 128), "z", 0, 0, tiled=True)
    coef = pl.pallas_call(
        merge_z_kernel,
        out_shape=f32(z * COEFS, 128),
        in_specs=[VMEM],
        out_specs=VMEM,
        compiler_params=SMALL,
        name="merge_z",
    )(stats.reshape(z * STATS, 128))
    coef = lax.all_to_all(coef.reshape(z, COEFS, 1, 128), "z", 0, 0, tiled=True)
    coef = pl.pallas_call(
        spread_kernel,
        out_shape=f32(X, COEFS, 8, cols),
        in_specs=[VMEM],
        out_specs=VMEM,
        compiler_params=SMALL,
        name="spread",
    )(coef.reshape(z * COEFS, 128))
    coef = lax.all_to_all(coef, "x", 0, 0, tiled=True)
    return pl.pallas_call(
        apply_kernel,
        out_shape=f32(LOCAL, FIELDS, rows, cols),
        in_specs=[VMEM] * 3,
        out_specs=VMEM,
        compiler_params=LARGE,
        name="apply",
    )(coef, inner_field, edge_field)


def solution(mesh):
    devices = mesh.devices
    fine = Mesh(devices.reshape(devices.shape[0] // X, X, devices.shape[1]), ("z", "x", "space"))
    member = ("z", "x")
    in_specs = (
        P(member, None, "space", None),
        P("space", None),
        P("space", None),
        P(None, "space", None),
        P(None, "space", None),
        P(None, "space", None),
        P(),
        P("space"),
    )
    out_specs = P(member, None, "space", None)
    return jax.shard_map(body, mesh=fine, in_specs=in_specs, out_specs=out_specs, check_vma=False)
```

```python
import jax
import jax.numpy as jnp
from jax import lax
from jax.experimental import pallas as pl
from jax.experimental.pallas import tpu as pltpu
from jax.sharding import Mesh, PartitionSpec as P

STEPS = 4
RADIUS = 4
LOCAL = 8
FIELDS = 3
X = 4
HALO = 8
STATS = 19
COEFS = 9

jitter = 0.05
pair_list = ((0, 0), (1, 0), (1, 1), (2, 0), (2, 1), (2, 2))
VMEM = pl.BlockSpec(memory_space=pltpu.VMEM)
HBM = pl.BlockSpec(memory_space=pltpu.HBM)

LARGE = pltpu.CompilerParams(vmem_limit_bytes=8 << 20)
SMALL = pltpu.CompilerParams(vmem_limit_bytes=2 << 20)


def cholesky_rows(matrix):
    first = jnp.sqrt(matrix[0])
    second = matrix[1] / first
    fourth = matrix[3] / first
    third = jnp.sqrt(matrix[2] - second * second)
    fifth = (matrix[4] - fourth * second) / third
    sixth = jnp.sqrt(matrix[5] - fourth * fourth - fifth * fifth)
    return [first, second, third, fourth, fifth, sixth]


def lower_inverse(packed):
    head = 1.0 / packed[0]
    middle = 1.0 / packed[2]
    tail = 1.0 / packed[5]
    below_head = -packed[1] * head * middle
    below_middle = -packed[4] * middle * tail
    corner = -(packed[3] * head + packed[4] * below_head) * tail
    return [head, below_head, middle, corner, below_middle, tail]


def lower_product(left_side, right_side):
    return [
        left_side[0] * right_side[0],
        left_side[1] * right_side[0] + left_side[2] * right_side[1],
        left_side[2] * right_side[2],
        left_side[3] * right_side[0] + left_side[4] * right_side[1] + left_side[5] * right_side[3],
        left_side[4] * right_side[2] + left_side[5] * right_side[4],
        left_side[5] * right_side[5],
    ]


HALF = 128
PAD = 8
MOVING = 8


def selection(back):
    i = lax.broadcasted_iota(jnp.int32, (2 * HALF, 2 * HALF), 1 if back else 0)
    j = lax.broadcasted_iota(jnp.int32, (2 * HALF, 2 * HALF), 0 if back else 1)
    source = jnp.where(j < HALF, 2 * j, 2 * (j - HALF) + 1)
    return jnp.where(i == source, 1.0, 0.0).astype(jnp.bfloat16)


def rearranged(value, matrix):
    high = value.astype(jnp.bfloat16)
    rest = value - high.astype(jnp.float32)
    middle = rest.astype(jnp.bfloat16)
    low = (rest - middle.astype(jnp.float32)).astype(jnp.bfloat16)
    out = None
    for part in (high, middle, low):
        term = jnp.dot(part, matrix, preferred_element_type=jnp.float32)
        out = term if out is None else out + term
    return out


def turned(value, k):
    return pltpu.roll(value, k % HALF, 1)


def advance(pair, buffer_ref, coef_ref):
    rows = pair[0].shape[0]
    for step in range(STEPS):
        slot = buffer_ref.at[step % 2]
        for h in range(2):
            slot[h, PAD : PAD + rows] = pair[h]
        even, odd = pair
        sides = (odd + turned(odd, 1), even + turned(even, -1))
        pair = tuple(
            coef_ref[0, h] * pair[h]
            + coef_ref[1, h] * slot[h, PAD - 1 : PAD - 1 + rows]
            + coef_ref[2, h] * (slot[h, PAD + 1 : PAD + 1 + rows] + sides[h])
            for h in range(2)
        )
    return pair


def radius_weights(radii_ref, rows):
    radii = [jnp.concatenate([radii_ref[f]] * (rows // 8), axis=0) for f in range(FIELDS)]
    return [
        [None, None] + [jnp.where(r >= float(k), 1.0, 0.0) for k in range(2, RADIUS + 1)]
        for r in radii
    ]


def row_total(likelihood_ref, start, rows, weights):
    def both(k):
        return (
            likelihood_ref[start - k : start - k + rows]
            + likelihood_ref[start + k : start + k + rows]
        )

    outer = both(RADIUS)
    for k in range(RADIUS - 1, 0, -1):
        outer = both(k) + weights[k + 1] * outer
    return likelihood_ref[start : start + rows] + outer


def column_total(totals, weights):
    def mix():
        return tuple(sum((t[h] for t in totals[1:]), totals[0][h]) for h in range(2))

    mixed = [mix()] * 2
    for k in range(2, RADIUS + 1):
        totals = [tuple(weights[f][k] * t for t in totals[f]) for f in range(FIELDS)]
        mixed.append(mix())
    (even1, odd1), (even2, odd2), (even3, odd3), (even4, odd4) = mixed[1:]
    even = (
        (even1 + odd1)
        + (turned(even2 + odd1, 1) + turned(even2 + odd3, -1))
        + (turned(even4 + odd3, 2) + turned(even4, -2))
    )
    odd = (
        (odd1 + even1)
        + (turned(odd2 + even3, 1) + turned(odd2 + even1, -1))
        + (turned(odd4, 2) + turned(odd4 + even3, -2))
    )
    return even, odd


def local_statistics(scores, cells):
    def plus(terms):
        return sum(terms[1:], terms[0])

    peak = scores[0]
    for s in scores[1:]:
        peak = jnp.maximum(peak, s)
    importance = [jnp.exp(s - peak) for s in scores]
    total = plus(importance)
    inverse = 1.0 / total
    share = 1.0 / LOCAL
    center = [plus([c[f] for c in cells]) * share for f in range(FIELDS)]
    away = [[c[f] - center[f] for f in range(FIELDS)] for c in cells]
    drift = [
        plus([w * a[f] for w, a in zip(importance, away)]) * inverse for f in range(FIELDS)
    ]
    post, prior = [], []
    for i, j in pair_list:
        products = [a[i] * a[j] for a in away]
        prior.append(plus(products) * share)
        post.append(
            plus([w * p for w, p in zip(importance, products)]) * inverse - drift[i] * drift[j]
        )
    moved = [center[f] + drift[f] for f in range(FIELDS)]
    return [peak + jnp.log(total)] + moved + post + center + prior


def pack_kernel(
    radius_hbm, temper_hbm, fields_hbm, spread_hbm, flow_hbm, quantity_hbm, confidence_hbm,
    mask_hbm, own_ref, last_ref, leading_ref, par_ref, tempering_ref, radii_ref,
    radius_ref, temper_ref, confidence_ref, mask_ref, sems,
):
    planes, rows = fields_hbm.shape[:2]
    tail = pl.ds(rows - HALO, HALO)
    head = pl.ds(0, HALO)
    sent = pl.ds(0, planes)
    pairs = (
        (confidence_hbm, confidence_ref),
        (mask_hbm, mask_ref),
        (spread_hbm, par_ref.at[0]),
        (flow_hbm, par_ref.at[1]),
        (quantity_hbm, par_ref.at[pl.ds(2, FIELDS)]),
        (temper_hbm, temper_ref),
        (radius_hbm, radius_ref),
        (fields_hbm.at[:, tail], last_ref.at[sent]),
        (fields_hbm.at[:, head], leading_ref.at[sent]),
        (fields_hbm, own_ref),
    )
    copies = [
        pltpu.make_async_copy(source, target, sems.at[number])
        for number, (source, target) in enumerate(pairs)
    ]
    for copy in copies:
        copy.start()
    for copy in copies[:7]:
        copy.wait()
    for f in range(FIELDS):
        par_ref[5 + f] = -0.5 * mask_ref[f].astype(jnp.float32) * confidence_ref[f]
        radius = radius_ref[:, f : f + 1].astype(jnp.float32)
        radii_ref[f] = jnp.broadcast_to(radius, (8, HALF))
    for p in range(MOVING):
        last_ref[planes + p] = par_ref[p, tail]
        leading_ref[planes + p] = par_ref[p, head]
    row = lax.broadcasted_iota(jnp.int32, (rows, rows), 0)
    column = lax.broadcasted_iota(jnp.int32, (rows, rows), 1)
    along = jnp.broadcast_to(temper_ref[...].astype(jnp.float32), (rows, rows))
    each = jnp.sum(jnp.where(row == column, along, 0.0), axis=1, keepdims=True)
    tempering_ref[...] = jnp.exp2(-jnp.broadcast_to(each, (rows, HALF)))
    for copy in copies[7:]:
        copy.wait()


def interior_kernel(
    own_ref, par_ref, temper_ref, radii_ref, field_ref, stats_ref, split_ref, split_par_ref,
    coef_ref, buffer_ref, likelihood_ref, score_ref,
):
    rows = own_ref.shape[1]
    inner = rows - 16
    matrix = selection(False)
    for source, target in (
        (par_ref[...], split_par_ref),
        (own_ref[...], split_ref),
    ):
        moved = rearranged(source.reshape(-1, 2 * HALF), matrix)
        for p in range(moved.shape[0] // rows):
            for h in range(2):
                target[p, h] = moved[p * rows : (p + 1) * rows, h * HALF : (h + 1) * HALF]
    for h in range(2):
        spread, flow = split_par_ref[0, h], split_par_ref[1, h]
        coef_ref[0, h] = 1.0 - 4.0 * spread - flow
        coef_ref[1, h] = spread + flow
        coef_ref[2, h] = spread
    weights = radius_weights(radii_ref, inner)

    def one_member(m, carry):
        totals = []
        for f in range(FIELDS):
            plane = m * FIELDS + f
            pair = advance(
                (split_ref[plane, 0], split_ref[plane, 1]), buffer_ref.at[f], coef_ref
            )
            for h in range(2):
                field_ref[m, f, h] = pair[h]
                misfit = pair[h] - split_par_ref[2 + f, h]
                likelihood_ref[f, h] = split_par_ref[5 + f, h] * misfit * misfit
            totals.append(
                tuple(row_total(likelihood_ref.at[f, h], 8, inner, weights[f]) for h in range(2))
            )
        score = column_total(totals, weights)
        for h in range(2):
            score_ref[m, h] = temper_ref[8 : 8 + inner] * score[h]
        return carry

    lax.fori_loop(0, LOCAL, one_member, 0)

    def one_group(g, carry):
        sub = pl.ds(pl.multiple_of(g * 8, 8), 8)
        deep = pl.ds(pl.multiple_of(g * 8 + 8, 8), 8)
        for h in range(2):
            scores = [score_ref[m, h, sub] for m in range(LOCAL)]
            cells = [[field_ref[m, f, h, deep] for f in range(FIELDS)] for m in range(LOCAL)]
            for number, value in enumerate(local_statistics(scores, cells)):
                stats_ref[g, number, :, h * HALF : (h + 1) * HALF] = value
        return carry

    lax.fori_loop(0, inner // 8, one_group, 0)


def edge_kernel(
    above_ref, below_ref, temper_ref, radii_ref, inner_field_ref, inner_stats_ref, split_ref,
    split_par_ref, field_ref, stats_ref, halo_ref, coef_ref, buffer_ref, par_ref, wide_ref,
    likelihood_ref, score_ref,
):
    rows = split_ref.shape[2]
    ends = (slice(0, 8), slice(rows - 8, rows))
    base = FIELDS * LOCAL
    for g in range(rows // 8 - 2):
        stats_ref[1 + g] = inner_stats_ref[g]

    def framed(end, own, halo):
        return jnp.concatenate([halo, own] if end == 0 else [own, halo], axis=0)

    matrix = selection(False)
    for end in range(2):
        source = (above_ref, below_ref)[end]
        moved = rearranged(source[...].reshape(-1, 2 * HALF), matrix)
        for p in range(base + MOVING):
            for h in range(2):
                halo_ref[end, p, h] = moved[p * 8 : (p + 1) * 8, h * HALF : (h + 1) * HALF]
    for end in range(2):
        for h in range(2):
            spread = framed(end, split_par_ref[0, h, ends[end]], halo_ref[end, base, h])
            flow = framed(end, split_par_ref[1, h, ends[end]], halo_ref[end, base + 1, h])
            coef_ref[end, 0, h] = 1.0 - 4.0 * spread - flow
            coef_ref[end, 1, h] = spread + flow
            coef_ref[end, 2, h] = spread
    for p in range(6):
        for h in range(2):
            par_ref[p, h, 0:8] = halo_ref[0, base + 2 + p, h]
            par_ref[p, h, 8 : 8 + rows] = split_par_ref[2 + p, h]
            par_ref[p, h, 8 + rows : 16 + rows] = halo_ref[1, base + 2 + p, h]
    weights = radius_weights(radii_ref, 8)

    def one_member(m, carry):
        for end in range(2):
            first = (4, rows - 4)[end]
            totals = []
            for f in range(FIELDS):
                plane = m * FIELDS + f
                start = tuple(
                    framed(end, split_ref[plane, h, ends[end]], halo_ref[end, plane, h])
                    for h in range(2)
                )
                pair = advance(start, buffer_ref.at[end, f], coef_ref.at[end])
                total = []
                for h in range(2):
                    wide = wide_ref.at[end, f, h]
                    fresh = buffer_ref.at[end, f, 0, h]
                    fresh[PAD : PAD + 16] = pair[h]
                    new = fresh[PAD + 4 : PAD + 12]
                    old = inner_field_ref[m, f, h, (4, rows - 12)[end] : (12, rows - 4)[end]]
                    wide[0:8] = (new, old)[end]
                    wide[8:16] = (old, new)[end]
                    field_ref[m, f, end, h] = wide[4:12]
                    misfit = framed(end, old, new) - par_ref[f, h, first : first + 16]
                    like = likelihood_ref.at[end, f, h]
                    like[...] = par_ref[3 + f, h, first : first + 16] * misfit * misfit
                    total.append(row_total(like, 4, 8, weights[f]))
                totals.append(tuple(total))
            score = column_total(totals, weights)
            for h in range(2):
                score_ref[m, end, h] = temper_ref[ends[end]] * score[h]
        return carry

    lax.fori_loop(0, LOCAL, one_member, 0)

    def one_half(h, carry):
        lane = pl.ds(pl.multiple_of(h * HALF, HALF), HALF)
        for end in range(2):
            scores = [score_ref[m, end, h] for m in range(LOCAL)]
            cells = [[field_ref[m, f, end, h] for f in range(FIELDS)] for m in range(LOCAL)]
            for number, value in enumerate(local_statistics(scores, cells)):
                stats_ref[(0, rows // 8 - 1)[end], number, :, lane] = value
        return carry

    lax.fori_loop(0, 2, one_half, 0)


def merged(parts, add, biggest):
    peak = biggest(parts[0])
    mass = [jnp.exp(p - peak) for p in parts[0]]
    total = add(mass)
    out = [peak + jnp.log(total)]
    for first, weights in ((1, mass), (10, None)):
        count = len(mass)

        def average(terms):
            if weights is None:
                return add(terms)
            return add([weights[s] * terms[s] for s in range(count)])

        share = 1.0 / (total if weights is not None else add([jnp.ones_like(m) for m in mass]))
        means = [average(parts[first + f]) * share for f in range(FIELDS)]
        away = [[parts[first + f][s] - means[f] for s in range(count)] for f in range(FIELDS)]
        out += means
        for number, (i, j) in enumerate(pair_list):
            second = parts[first + FIELDS + number]
            out.append(
                average([second[s] + away[i][s] * away[j][s] for s in range(count)]) * share
            )
    return out


def merge_x_kernel(part_ref, out_ref):
    def add(terms):
        return sum(terms[1:], terms[0])

    def biggest(terms):
        peak = terms[0]
        for t in terms[1:]:
            peak = jnp.maximum(peak, t)
        return peak

    for half in range(2):
        lane = pl.ds(half * 128, 128)
        parts = [[part_ref[s, p, :, lane] for s in range(X)] for p in range(STATS)]
        out = merged(parts, add, biggest)
        for p in range(STATS):
            out_ref[pl.ds(half * 8 * STATS + p, 8, stride=STATS), :] = out[p]


def merge_z_kernel(part_ref, out_ref):
    sources = part_ref.shape[0] // STATS
    blocks = sources // 8

    def add(terms):
        return jnp.sum(sum(terms[1:], terms[0]), axis=0, keepdims=True)

    def biggest(terms):
        peak = terms[0]
        for t in terms[1:]:
            peak = jnp.maximum(peak, t)
        return jnp.max(peak, axis=0, keepdims=True)

    parts = [
        [part_ref[pl.ds(b * 8 * STATS + p, 8, stride=STATS), :] for b in range(blocks)]
        for p in range(STATS)
    ]
    out = merged(parts, add, biggest)
    diagonal = (0, 2, 5)
    post_cov = [out[4 + n] + (jitter if n in diagonal else 0.0) for n in range(6)]
    prior_cov = [out[13 + n] + (jitter if n in diagonal else 0.0) for n in range(6)]
    gain = lower_product(cholesky_rows(post_cov), lower_inverse(cholesky_rows(prior_cov)))
    result = list(gain)
    for row in range(FIELDS):
        running = out[1 + row]
        for source in range(row + 1):
            running = running - gain[row * (row + 1) // 2 + source] * out[10 + source]
        result.append(running)
    for p in range(COEFS):
        value = jnp.broadcast_to(result[p], (8, 128))
        for b in range(blocks):
            out_ref[pl.ds(b * 8 * COEFS + p, 8, stride=COEFS), :] = value


def spread_kernel(coef_ref, out_ref):
    for half in range(2):
        lane = pl.ds(half * HALF, HALF)
        for p in range(COEFS):
            value = coef_ref[pl.ds(half * 8 * COEFS + p, 8, stride=COEFS), :]
            for target in range(X):
                out_ref[target, p, :, lane] = value


def apply_kernel(coef_ref, inner_ref, edge_ref, out_ref):
    matrix = selection(True)
    rows = inner_ref.shape[3]
    last = X - 1
    for m in range(LOCAL):
        result = [[[None] * 2 for _ in range(X)] for _ in range(FIELDS)]
        for g in range(X):
            for h in range(2):
                lane = slice(h * HALF, (h + 1) * HALF)
                if g in (0, last):
                    cells = [edge_ref[m, f, 0 if g == 0 else 1, h] for f in range(FIELDS)]
                else:
                    cells = [inner_ref[m, f, h, g * 8 : g * 8 + 8] for f in range(FIELDS)]
                for row in range(FIELDS):
                    running = coef_ref[g, 6 + row, :, lane]
                    for source in range(row + 1):
                        entry = coef_ref[g, row * (row + 1) // 2 + source, :, lane]
                        running = running + entry * cells[source]
                    result[row][g][h] = running
        stacked = jnp.concatenate(
            [jnp.concatenate(pair, axis=1) for row in result for pair in row], axis=0
        )
        stacked = rearranged(stacked, matrix)
        for row in range(FIELDS):
            out_ref[m, row] = stacked[row * rows : (row + 1) * rows]


def f32(*shape):
    return jax.ShapeDtypeStruct(shape, jnp.float32)


def body(
    sample_group,
    spreading_ratio,
    flow_ratio,
    measured_quantity,
    measured_confidence,
    obs_mask,
    radius,
    temper,
):
    rows, cols = sample_group.shape[2:]
    z = lax.axis_size("z")
    sent = LOCAL * FIELDS + MOVING
    own, last, leading, own_par, tempering, radii = pl.pallas_call(
        pack_kernel,
        out_shape=(
            f32(LOCAL * FIELDS, rows, cols),
            f32(sent, HALO, cols),
            f32(sent, HALO, cols),
            f32(MOVING, rows, cols),
            f32(rows, HALF),
            f32(FIELDS, 8, HALF),
        ),
        in_specs=[HBM] * 8,
        out_specs=(VMEM,) * 6,
        scratch_shapes=[
            pltpu.VMEM((1, FIELDS), jnp.int32),
            pltpu.VMEM((1, rows), jnp.int32),
            pltpu.VMEM((FIELDS, rows, cols), jnp.float32),
            pltpu.VMEM((FIELDS, rows, cols), jnp.int32),
            pltpu.SemaphoreType.DMA((10,)),
        ],
        compiler_params=LARGE,
        name="pack",
    )(
        *(
            pltpu.with_memory_space_constraint(array, pltpu.HBM)
            for array in (
                radius.reshape(1, FIELDS),
                temper.reshape(1, rows),
                sample_group.reshape(LOCAL * FIELDS, rows, cols),
                spreading_ratio,
                flow_ratio,
                measured_quantity,
                measured_confidence,
                obs_mask,
            )
        )
    )
    count = lax.axis_size("space")
    up = [(i, (i + 1) % count) for i in range(count)]
    down = [(j, i) for i, j in up]
    above = lax.ppermute(last, "space", up)
    below = lax.ppermute(leading, "space", down)
    inner_field, inner_stats, split, split_par = pl.pallas_call(
        interior_kernel,
        out_shape=(
            f32(LOCAL, FIELDS, 2, rows, HALF),
            f32(rows // 8 - 2, STATS, 8, cols),
            f32(LOCAL * FIELDS, 2, rows, HALF),
            f32(MOVING, 2, rows, HALF),
        ),
        in_specs=[VMEM] * 4,
        out_specs=(VMEM,) * 4,
        scratch_shapes=[
            pltpu.VMEM((3, 2, rows, HALF), jnp.float32),
            pltpu.VMEM((FIELDS, 2, 2, rows + 2 * PAD, HALF), jnp.float32),
            pltpu.VMEM((FIELDS, 2, rows, HALF), jnp.float32),
            pltpu.VMEM((LOCAL, 2, rows - 16, HALF), jnp.float32),
        ],
        compiler_params=LARGE,
        name="interior",
    )(own, own_par, tempering, radii)

    edge_field, stats = pl.pallas_call(
        edge_kernel,
        out_shape=(f32(LOCAL, FIELDS, 2, 2, 8, HALF), f32(X, STATS, 8, cols)),
        in_specs=[VMEM] * 8,
        out_specs=(VMEM, VMEM),
        scratch_shapes=[
            pltpu.VMEM((2, LOCAL * FIELDS + MOVING, 2, 8, HALF), jnp.float32),
            pltpu.VMEM((2, 3, 2, 16, HALF), jnp.float32),
            pltpu.VMEM((2, FIELDS, 2, 2, 16 + 2 * PAD, HALF), jnp.float32),
            pltpu.VMEM((6, 2, rows + 16, HALF), jnp.float32),
            pltpu.VMEM((2, FIELDS, 2, 16, HALF), jnp.float32),
            pltpu.VMEM((2, FIELDS, 2, 16, HALF), jnp.float32),
            pltpu.VMEM((LOCAL, 2, 2, 8, HALF), jnp.float32),
        ],
        compiler_params=LARGE,
        name="edge",
    )(above, below, tempering, radii, inner_field, inner_stats, split, split_par)

    stats = lax.all_to_all(stats, "x", 0, 0, tiled=True)
    stats = pl.pallas_call(
        merge_x_kernel,
        out_shape=f32(z * STATS, 128),
        in_specs=[VMEM],
        out_specs=VMEM,
        compiler_params=SMALL,
        name="merge_x",
    )(stats)
    stats = lax.all_to_all(stats.reshape(z, STATS, 1, 128), "z", 0, 0, tiled=True)
    coef = pl.pallas_call(
        merge_z_kernel,
        out_shape=f32(z * COEFS, 128),
        in_specs=[VMEM],
        out_specs=VMEM,
        compiler_params=SMALL,
        name="merge_z",
    )(stats.reshape(z * STATS, 128))
    coef = lax.all_to_all(coef.reshape(z, COEFS, 1, 128), "z", 0, 0, tiled=True)
    coef = pl.pallas_call(
        spread_kernel,
        out_shape=f32(X, COEFS, 8, cols),
        in_specs=[VMEM],
        out_specs=VMEM,
        compiler_params=SMALL,
        name="spread",
    )(coef.reshape(z * COEFS, 128))
    coef = lax.all_to_all(coef, "x", 0, 0, tiled=True)
    return pl.pallas_call(
        apply_kernel,
        out_shape=f32(LOCAL, FIELDS, rows, cols),
        in_specs=[VMEM] * 3,
        out_specs=VMEM,
        compiler_params=LARGE,
        name="apply",
    )(coef, inner_field, edge_field)


def solution(mesh):
    devices = mesh.devices
    fine = Mesh(devices.reshape(devices.shape[0] // X, X, devices.shape[1]), ("z", "x", "space"))
    member = ("z", "x")
    in_specs = (
        P(member, None, "space", None),
        P("space", None),
        P("space", None),
        P(None, "space", None),
        P(None, "space", None),
        P(None, "space", None),
        P(),
        P("space"),
    )
    out_specs = P(member, None, "space", None)
    return jax.shard_map(body, mesh=fine, in_specs=in_specs, out_specs=out_specs, check_vma=False)
```

```python
import jax
import jax.numpy as jnp
from jax import lax
from jax.experimental import pallas as pl
from jax.experimental.pallas import tpu as pltpu
from jax.sharding import Mesh, PartitionSpec as P

STEPS = 4
RADIUS = 4
LOCAL = 8
FIELDS = 3
X = 4
HALO = 8
STATS = 19
COEFS = 9

jitter = 0.05
pair_list = ((0, 0), (1, 0), (1, 1), (2, 0), (2, 1), (2, 2))
VMEM = pl.BlockSpec(memory_space=pltpu.VMEM)
HBM = pl.BlockSpec(memory_space=pltpu.HBM)

LARGE = pltpu.CompilerParams(vmem_limit_bytes=8 << 20)
SMALL = pltpu.CompilerParams(vmem_limit_bytes=2 << 20)


def cholesky_rows(matrix):
    first = jnp.sqrt(matrix[0])
    second = matrix[1] / first
    fourth = matrix[3] / first
    third = jnp.sqrt(matrix[2] - second * second)
    fifth = (matrix[4] - fourth * second) / third
    sixth = jnp.sqrt(matrix[5] - fourth * fourth - fifth * fifth)
    return [first, second, third, fourth, fifth, sixth]


def lower_inverse(packed):
    head = 1.0 / packed[0]
    middle = 1.0 / packed[2]
    tail = 1.0 / packed[5]
    below_head = -packed[1] * head * middle
    below_middle = -packed[4] * middle * tail
    corner = -(packed[3] * head + packed[4] * below_head) * tail
    return [head, below_head, middle, corner, below_middle, tail]


def lower_product(left_side, right_side):
    return [
        left_side[0] * right_side[0],
        left_side[1] * right_side[0] + left_side[2] * right_side[1],
        left_side[2] * right_side[2],
        left_side[3] * right_side[0] + left_side[4] * right_side[1] + left_side[5] * right_side[3],
        left_side[4] * right_side[2] + left_side[5] * right_side[4],
        left_side[5] * right_side[5],
    ]


HALF = 128
PAD = 8
TOGETHER = 8
MOVING = 8


def split(value):
    return value[:, :HALF], value[:, HALF:]


def lane_sides(pair, k):
    a, b = pair
    lane = lax.broadcasted_iota(jnp.int32, a.shape, 1)
    low, high = lane < k, lane >= HALF - k
    left_a, left_b = pltpu.roll(a, k, 1), pltpu.roll(b, k, 1)
    right_a, right_b = pltpu.roll(a, HALF - k, 1), pltpu.roll(b, HALF - k, 1)
    return (
        jnp.where(low, left_b, left_a) + jnp.where(high, right_b, right_a),
        jnp.where(low, left_a, left_b) + jnp.where(high, right_a, right_b),
    )


def advance(pairs, buffers, coefs):
    rows = pairs[0][0].shape[0]
    for step in range(STEPS):
        slots = [b.at[step % 2] for b in buffers]
        for slot, pair in zip(slots, pairs):
            for h in range(2):
                slot[h, PAD : PAD + rows] = pair[h]
        after = []
        for slot, pair, coef in zip(slots, pairs, coefs):
            sides = lane_sides(pair, 1)
            after.append(
                tuple(
                    coef[0, h] * pair[h]
                    + coef[1, h] * slot[h, PAD - 1 : PAD - 1 + rows]
                    + coef[2, h] * (slot[h, PAD + 1 : PAD + 1 + rows] + sides[h])
                    for h in range(2)
                )
            )
        pairs = after
    return pairs


def radius_weights(radii_ref, rows):
    radii = [jnp.concatenate([radii_ref[f]] * (rows // 8), axis=0) for f in range(FIELDS)]
    return [
        [None, None] + [jnp.where(r >= float(k), 1.0, 0.0) for k in range(2, RADIUS + 1)]
        for r in radii
    ]


def row_total(likelihood_ref, start, rows, weights):
    def both(k):
        return (
            likelihood_ref[start - k : start - k + rows]
            + likelihood_ref[start + k : start + k + rows]
        )

    outer = both(RADIUS)
    for k in range(RADIUS - 1, 0, -1):
        outer = both(k) + weights[k + 1] * outer
    return likelihood_ref[start : start + rows] + outer


def column_total(totals, weights):
    score = tuple(sum((t[h] for t in totals[1:]), totals[0][h]) for h in range(2))
    mixed = score
    for k in range(1, RADIUS + 1):
        if k > 1:
            totals = [
                tuple(weights[f][k] * t for t in totals[f]) for f in range(FIELDS)
            ]
            mixed = tuple(sum((t[h] for t in totals[1:]), totals[0][h]) for h in range(2))
        sides = lane_sides(mixed, k)
        score = tuple(score[h] + sides[h] for h in range(2))
    return score


def local_statistics(scores, cells):
    def plus(terms):
        return sum(terms[1:], terms[0])

    peak = scores[0]
    for s in scores[1:]:
        peak = jnp.maximum(peak, s)
    importance = [jnp.exp(s - peak) for s in scores]
    total = plus(importance)
    inverse = 1.0 / total
    share = 1.0 / LOCAL
    center = [plus([c[f] for c in cells]) * share for f in range(FIELDS)]
    away = [[c[f] - center[f] for f in range(FIELDS)] for c in cells]
    drift = [
        plus([w * a[f] for w, a in zip(importance, away)]) * inverse for f in range(FIELDS)
    ]
    post, prior = [], []
    for i, j in pair_list:
        products = [a[i] * a[j] for a in away]
        prior.append(plus(products) * share)
        post.append(
            plus([w * p for w, p in zip(importance, products)]) * inverse - drift[i] * drift[j]
        )
    moved = [center[f] + drift[f] for f in range(FIELDS)]
    return [peak + jnp.log(total)] + moved + post + center + prior


def pack_kernel(
    radius_hbm, temper_hbm, fields_hbm, spread_hbm, flow_hbm, quantity_hbm, confidence_hbm,
    mask_hbm, own_ref, last_ref, leading_ref, par_ref, tempering_ref, radii_ref,
    radius_ref, temper_ref, confidence_ref, mask_ref, sems,
):
    planes, rows = fields_hbm.shape[:2]
    tail = pl.ds(rows - HALO, HALO)
    head = pl.ds(0, HALO)
    sent = pl.ds(0, planes)
    pairs = (
        (confidence_hbm, confidence_ref),
        (mask_hbm, mask_ref),
        (spread_hbm, par_ref.at[0]),
        (flow_hbm, par_ref.at[1]),
        (quantity_hbm, par_ref.at[pl.ds(2, FIELDS)]),
        (temper_hbm, temper_ref),
        (radius_hbm, radius_ref),
        (fields_hbm.at[:, tail], last_ref.at[sent]),
        (fields_hbm.at[:, head], leading_ref.at[sent]),
        (fields_hbm, own_ref),
    )
    copies = [
        pltpu.make_async_copy(source, target, sems.at[number])
        for number, (source, target) in enumerate(pairs)
    ]
    for copy in copies:
        copy.start()
    for copy in copies[:7]:
        copy.wait()
    for f in range(FIELDS):
        par_ref[5 + f] = -0.5 * mask_ref[f].astype(jnp.float32) * confidence_ref[f]
        radius = radius_ref[:, f : f + 1].astype(jnp.float32)
        radii_ref[f] = jnp.broadcast_to(radius, (8, HALF))
    for p in range(MOVING):
        last_ref[planes + p] = par_ref[p, tail]
        leading_ref[planes + p] = par_ref[p, head]
    row = lax.broadcasted_iota(jnp.int32, (rows, rows), 0)
    column = lax.broadcasted_iota(jnp.int32, (rows, rows), 1)
    along = jnp.broadcast_to(temper_ref[...].astype(jnp.float32), (rows, rows))
    each = jnp.sum(jnp.where(row == column, along, 0.0), axis=1, keepdims=True)
    tempering_ref[...] = jnp.exp2(-jnp.broadcast_to(each, (rows, HALF)))
    for copy in copies[7:]:
        copy.wait()


def interior_kernel(
    own_ref, par_ref, temper_ref, radii_ref, field_ref, stats_ref,
    coef_ref, buffer_ref, likelihood_ref, score_ref,
):
    rows = own_ref.shape[1]
    inner = rows - 16
    spread, flow = split(par_ref[0]), split(par_ref[1])
    for h in range(2):
        coef_ref[0, h] = 1.0 - 4.0 * spread[h] - flow[h]
        coef_ref[1, h] = spread[h] + flow[h]
        coef_ref[2, h] = spread[h]
    weights = radius_weights(radii_ref, inner)

    def some_members(step, carry):
        first = step * TOGETHER
        planes = range(TOGETHER * FIELDS)
        pairs = advance(
            [split(own_ref[first * FIELDS + p]) for p in planes],
            [buffer_ref.at[p] for p in planes],
            [coef_ref] * len(planes),
        )
        for p in planes:
            f = p % FIELDS
            quantity, observed = split(par_ref[2 + f]), split(par_ref[5 + f])
            for h in range(2):
                field_ref[first + p // FIELDS, f, h] = pairs[p][h]
                misfit = pairs[p][h] - quantity[h]
                likelihood_ref[p, h] = observed[h] * misfit * misfit
        for u in range(TOGETHER):
            totals = [
                tuple(
                    row_total(likelihood_ref.at[u * FIELDS + f, h], 8, inner, weights[f])
                    for h in range(2)
                )
                for f in range(FIELDS)
            ]
            score = column_total(totals, weights)
            for h in range(2):
                score_ref[first + u, h] = temper_ref[8 : 8 + inner] * score[h]
        return carry

    lax.fori_loop(0, LOCAL // TOGETHER, some_members, 0)

    def one_group(g, carry):
        sub = pl.ds(pl.multiple_of(g * 8, 8), 8)
        deep = pl.ds(pl.multiple_of(g * 8 + 8, 8), 8)
        for h in range(2):
            scores = [score_ref[m, h, sub] for m in range(LOCAL)]
            cells = [[field_ref[m, f, h, deep] for f in range(FIELDS)] for m in range(LOCAL)]
            for number, value in enumerate(local_statistics(scores, cells)):
                stats_ref[g, number, :, h * HALF : (h + 1) * HALF] = value
        return carry

    lax.fori_loop(0, inner // 8, one_group, 0)


def edge_kernel(
    own_ref, above_ref, below_ref, own_par_ref, temper_ref, radii_ref, inner_field_ref,
    inner_stats_ref, field_ref, stats_ref, coef_ref, buffer_ref, par_ref, wide_ref,
    likelihood_ref, score_ref,
):
    rows = own_ref.shape[1]
    ends = (slice(0, 8), slice(rows - 8, rows))
    halos = (above_ref, below_ref)
    base = FIELDS * LOCAL
    for g in range(rows // 8 - 2):
        stats_ref[1 + g] = inner_stats_ref[g]

    def framed(end, own, halo):
        return jnp.concatenate([halo, own] if end == 0 else [own, halo], axis=0)

    for end in range(2):
        spread = split(framed(end, own_par_ref[0, ends[end]], halos[end][base]))
        flow = split(framed(end, own_par_ref[1, ends[end]], halos[end][base + 1]))
        for h in range(2):
            coef_ref[end, 0, h] = 1.0 - 4.0 * spread[h] - flow[h]
            coef_ref[end, 1, h] = spread[h] + flow[h]
            coef_ref[end, 2, h] = spread[h]
    for p in range(6):
        for h in range(2):
            lane = slice(h * HALF, (h + 1) * HALF)
            par_ref[p, h, 0:8] = above_ref[base + 2 + p, :, lane]
            par_ref[p, h, 8 : 8 + rows] = own_par_ref[2 + p, :, lane]
            par_ref[p, h, 8 + rows : 16 + rows] = below_ref[base + 2 + p, :, lane]
    weights = radius_weights(radii_ref, 8)

    def some_members(step, carry):
        first = step * TOGETHER
        jobs = [
            (end, p) for p in range(TOGETHER * FIELDS) for end in range(2)
        ]
        pairs = advance(
            [
                split(
                    framed(
                        end,
                        own_ref[first * FIELDS + p, ends[end]],
                        halos[end][first * FIELDS + p],
                    )
                )
                for end, p in jobs
            ],
            [buffer_ref.at[end, p] for end, p in jobs],
            [coef_ref.at[end] for end, p in jobs],
        )
        for (end, p), pair in zip(jobs, pairs):
            m, f = first + p // FIELDS, p % FIELDS
            start = (4, rows - 4)[end]
            for h in range(2):
                wide = wide_ref.at[end, p, h]
                fresh = buffer_ref.at[end, p, 0, h]
                fresh[PAD : PAD + 16] = pair[h]
                new = fresh[PAD + 4 : PAD + 12]
                old = inner_field_ref[m, f, h, (4, rows - 12)[end] : (12, rows - 4)[end]]
                wide[0:8] = (new, old)[end]
                wide[8:16] = (old, new)[end]
                field_ref[m, f, end, h] = wide[4:12]
                misfit = framed(end, old, new) - par_ref[f, h, start : start + 16]
                observed = par_ref[3 + f, h, start : start + 16]
                likelihood_ref[end, p, h] = observed * misfit * misfit
        for u in range(TOGETHER):
            for end in range(2):
                totals = [
                    tuple(
                        row_total(
                            likelihood_ref.at[end, u * FIELDS + f, h], 4, 8, weights[f]
                        )
                        for h in range(2)
                    )
                    for f in range(FIELDS)
                ]
                score = column_total(totals, weights)
                for h in range(2):
                    score_ref[first + u, end, h] = temper_ref[ends[end]] * score[h]
        return carry

    lax.fori_loop(0, LOCAL // TOGETHER, some_members, 0)

    def one_half(h, carry):
        lane = pl.ds(pl.multiple_of(h * HALF, HALF), HALF)
        for end in range(2):
            scores = [score_ref[m, end, h] for m in range(LOCAL)]
            cells = [[field_ref[m, f, end, h] for f in range(FIELDS)] for m in range(LOCAL)]
            for number, value in enumerate(local_statistics(scores, cells)):
                stats_ref[(0, rows // 8 - 1)[end], number, :, lane] = value
        return carry

    lax.fori_loop(0, 2, one_half, 0)


def merged(parts, add, biggest):
    peak = biggest(parts[0])
    mass = [jnp.exp(p - peak) for p in parts[0]]
    total = add(mass)
    out = [peak + jnp.log(total)]
    for first, weights in ((1, mass), (10, None)):
        count = len(mass)

        def average(terms):
            if weights is None:
                return add(terms)
            return add([weights[s] * terms[s] for s in range(count)])

        share = 1.0 / (total if weights is not None else add([jnp.ones_like(m) for m in mass]))
        means = [average(parts[first + f]) * share for f in range(FIELDS)]
        away = [[parts[first + f][s] - means[f] for s in range(count)] for f in range(FIELDS)]
        out += means
        for number, (i, j) in enumerate(pair_list):
            second = parts[first + FIELDS + number]
            out.append(
                average([second[s] + away[i][s] * away[j][s] for s in range(count)]) * share
            )
    return out


def merge_x_kernel(part_ref, out_ref):
    def add(terms):
        return sum(terms[1:], terms[0])

    def biggest(terms):
        peak = terms[0]
        for t in terms[1:]:
            peak = jnp.maximum(peak, t)
        return peak

    for half in range(2):
        lane = pl.ds(half * 128, 128)
        parts = [[part_ref[s, p, :, lane] for s in range(X)] for p in range(STATS)]
        out = merged(parts, add, biggest)
        for p in range(STATS):
            out_ref[pl.ds(half * 8 * STATS + p, 8, stride=STATS), :] = out[p]


def merge_z_kernel(part_ref, out_ref):
    sources = part_ref.shape[0] // STATS
    blocks = sources // 8

    def add(terms):
        return jnp.sum(sum(terms[1:], terms[0]), axis=0, keepdims=True)

    def biggest(terms):
        peak = terms[0]
        for t in terms[1:]:
            peak = jnp.maximum(peak, t)
        return jnp.max(peak, axis=0, keepdims=True)

    parts = [
        [part_ref[pl.ds(b * 8 * STATS + p, 8, stride=STATS), :] for b in range(blocks)]
        for p in range(STATS)
    ]
    out = merged(parts, add, biggest)
    diagonal = (0, 2, 5)
    post_cov = [out[4 + n] + (jitter if n in diagonal else 0.0) for n in range(6)]
    prior_cov = [out[13 + n] + (jitter if n in diagonal else 0.0) for n in range(6)]
    gain = lower_product(cholesky_rows(post_cov), lower_inverse(cholesky_rows(prior_cov)))
    result = list(gain)
    for row in range(FIELDS):
        running = out[1 + row]
        for source in range(row + 1):
            running = running - gain[row * (row + 1) // 2 + source] * out[10 + source]
        result.append(running)
    for p in range(COEFS):
        value = jnp.broadcast_to(result[p], (8, 128))
        for b in range(blocks):
            out_ref[pl.ds(b * 8 * COEFS + p, 8, stride=COEFS), :] = value


def spread_kernel(coef_ref, out_ref):
    for half in range(2):
        lane = pl.ds(half * HALF, HALF)
        for p in range(COEFS):
            value = coef_ref[pl.ds(half * 8 * COEFS + p, 8, stride=COEFS), :]
            for target in range(X):
                out_ref[target, p, :, lane] = value


def apply_kernel(coef_ref, inner_ref, edge_ref, out_ref):
    last = X - 1

    def one_member(m, carry):
        for g in range(X):
            for h in range(2):
                lane = slice(h * HALF, (h + 1) * HALF)
                if g in (0, last):
                    cells = [edge_ref[m, f, 0 if g == 0 else 1, h] for f in range(FIELDS)]
                else:
                    cells = [inner_ref[m, f, h, g * 8 : g * 8 + 8] for f in range(FIELDS)]
                for row in range(FIELDS):
                    running = coef_ref[g, 6 + row, :, lane]
                    for source in range(row + 1):
                        entry = coef_ref[g, row * (row + 1) // 2 + source, :, lane]
                        running = running + entry * cells[source]
                    out_ref[m, row, g * 8 : g * 8 + 8, lane] = running
        return carry

    lax.fori_loop(0, LOCAL, one_member, 0)


def f32(*shape):
    return jax.ShapeDtypeStruct(shape, jnp.float32)


def body(
    sample_group,
    spreading_ratio,
    flow_ratio,
    measured_quantity,
    measured_confidence,
    obs_mask,
    radius,
    temper,
):
    rows, cols = sample_group.shape[2:]
    z = lax.axis_size("z")
    sent = LOCAL * FIELDS + MOVING
    own, last, leading, own_par, tempering, radii = pl.pallas_call(
        pack_kernel,
        out_shape=(
            f32(LOCAL * FIELDS, rows, cols),
            f32(sent, HALO, cols),
            f32(sent, HALO, cols),
            f32(MOVING, rows, cols),
            f32(rows, HALF),
            f32(FIELDS, 8, HALF),
        ),
        in_specs=[HBM] * 8,
        out_specs=(VMEM,) * 6,
        scratch_shapes=[
            pltpu.VMEM((1, FIELDS), jnp.int32),
            pltpu.VMEM((1, rows), jnp.int32),
            pltpu.VMEM((FIELDS, rows, cols), jnp.float32),
            pltpu.VMEM((FIELDS, rows, cols), jnp.int32),
            pltpu.SemaphoreType.DMA((10,)),
        ],
        compiler_params=LARGE,
        name="pack",
    )(
        *(
            pltpu.with_memory_space_constraint(array, pltpu.HBM)
            for array in (
                radius.reshape(1, FIELDS),
                temper.reshape(1, rows),
                sample_group.reshape(LOCAL * FIELDS, rows, cols),
                spreading_ratio,
                flow_ratio,
                measured_quantity,
                measured_confidence,
                obs_mask,
            )
        )
    )
    count = lax.axis_size("space")
    up = [(i, (i + 1) % count) for i in range(count)]
    down = [(j, i) for i, j in up]
    above = lax.ppermute(last, "space", up)
    below = lax.ppermute(leading, "space", down)
    inner_field, inner_stats = pl.pallas_call(
        interior_kernel,
        out_shape=(f32(LOCAL, FIELDS, 2, rows, HALF), f32(rows // 8 - 2, STATS, 8, cols)),
        in_specs=[VMEM] * 4,
        out_specs=(VMEM, VMEM),
        scratch_shapes=[
            pltpu.VMEM((3, 2, rows, HALF), jnp.float32),
            pltpu.VMEM((TOGETHER * FIELDS, 2, 2, rows + 2 * PAD, HALF), jnp.float32),
            pltpu.VMEM((TOGETHER * FIELDS, 2, rows, HALF), jnp.float32),
            pltpu.VMEM((LOCAL, 2, rows - 16, HALF), jnp.float32),
        ],
        compiler_params=LARGE,
        name="interior",
    )(own, own_par, tempering, radii)

    edge_field, stats = pl.pallas_call(
        edge_kernel,
        out_shape=(f32(LOCAL, FIELDS, 2, 2, 8, HALF), f32(X, STATS, 8, cols)),
        in_specs=[VMEM] * 8,
        out_specs=(VMEM, VMEM),
        scratch_shapes=[
            pltpu.VMEM((2, 3, 2, 16, HALF), jnp.float32),
            pltpu.VMEM((2, TOGETHER * FIELDS, 2, 2, 16 + 2 * PAD, HALF), jnp.float32),
            pltpu.VMEM((6, 2, rows + 16, HALF), jnp.float32),
            pltpu.VMEM((2, TOGETHER * FIELDS, 2, 16, HALF), jnp.float32),
            pltpu.VMEM((2, TOGETHER * FIELDS, 2, 16, HALF), jnp.float32),
            pltpu.VMEM((LOCAL, 2, 2, 8, HALF), jnp.float32),
        ],
        compiler_params=LARGE,
        name="edge",
    )(own, above, below, own_par, tempering, radii, inner_field, inner_stats)

    stats = lax.all_to_all(stats, "x", 0, 0, tiled=True)
    stats = pl.pallas_call(
        merge_x_kernel,
        out_shape=f32(z * STATS, 128),
        in_specs=[VMEM],
        out_specs=VMEM,
        compiler_params=SMALL,
        name="merge_x",
    )(stats)
    stats = lax.all_to_all(stats.reshape(z, STATS, 1, 128), "z", 0, 0, tiled=True)
    coef = pl.pallas_call(
        merge_z_kernel,
        out_shape=f32(z * COEFS, 128),
        in_specs=[VMEM],
        out_specs=VMEM,
        compiler_params=SMALL,
        name="merge_z",
    )(stats.reshape(z * STATS, 128))
    coef = lax.all_to_all(coef.reshape(z, COEFS, 1, 128), "z", 0, 0, tiled=True)
    coef = pl.pallas_call(
        spread_kernel,
        out_shape=f32(X, COEFS, 8, cols),
        in_specs=[VMEM],
        out_specs=VMEM,
        compiler_params=SMALL,
        name="spread",
    )(coef.reshape(z * COEFS, 128))
    coef = lax.all_to_all(coef, "x", 0, 0, tiled=True)
    return pl.pallas_call(
        apply_kernel,
        out_shape=f32(LOCAL, FIELDS, rows, cols),
        in_specs=[VMEM] * 3,
        out_specs=VMEM,
        compiler_params=LARGE,
        name="apply",
    )(coef, inner_field, edge_field)


def solution(mesh):
    devices = mesh.devices
    fine = Mesh(devices.reshape(devices.shape[0] // X, X, devices.shape[1]), ("z", "x", "space"))
    member = ("z", "x")
    in_specs = (
        P(member, None, "space", None),
        P("space", None),
        P("space", None),
        P(None, "space", None),
        P(None, "space", None),
        P(None, "space", None),
        P(),
        P("space"),
    )
    out_specs = P(member, None, "space", None)
    return jax.shard_map(body, mesh=fine, in_specs=in_specs, out_specs=out_specs, check_vma=False)
```

```python
import jax
import jax.numpy as jnp
from jax import lax
from jax.experimental import pallas as pl
from jax.experimental.pallas import tpu as pltpu
from jax.sharding import Mesh, PartitionSpec as P

STEPS = 4
RADIUS = 4
LOCAL = 8
FIELDS = 3
X = 4
HALO = 8
STATS = 19
COEFS = 9

jitter = 0.05
pair_list = ((0, 0), (1, 0), (1, 1), (2, 0), (2, 1), (2, 2))
VMEM = pl.BlockSpec(memory_space=pltpu.VMEM)
HBM = pl.BlockSpec(memory_space=pltpu.HBM)

LARGE = pltpu.CompilerParams(vmem_limit_bytes=8 << 20)
SMALL = pltpu.CompilerParams(vmem_limit_bytes=2 << 20)


def cholesky_rows(matrix):
    first = jnp.sqrt(matrix[0])
    second = matrix[1] / first
    fourth = matrix[3] / first
    third = jnp.sqrt(matrix[2] - second * second)
    fifth = (matrix[4] - fourth * second) / third
    sixth = jnp.sqrt(matrix[5] - fourth * fourth - fifth * fifth)
    return [first, second, third, fourth, fifth, sixth]


def lower_inverse(packed):
    head = 1.0 / packed[0]
    middle = 1.0 / packed[2]
    tail = 1.0 / packed[5]
    below_head = -packed[1] * head * middle
    below_middle = -packed[4] * middle * tail
    corner = -(packed[3] * head + packed[4] * below_head) * tail
    return [head, below_head, middle, corner, below_middle, tail]


def lower_product(left_side, right_side):
    return [
        left_side[0] * right_side[0],
        left_side[1] * right_side[0] + left_side[2] * right_side[1],
        left_side[2] * right_side[2],
        left_side[3] * right_side[0] + left_side[4] * right_side[1] + left_side[5] * right_side[3],
        left_side[4] * right_side[2] + left_side[5] * right_side[4],
        left_side[5] * right_side[5],
    ]


HALF = 128
PAD = 8
TOGETHER = 8
MOVING = 8


def split(value):
    return value[:, :HALF], value[:, HALF:]


def lane_sides(pair, k):
    a, b = pair
    lane = lax.broadcasted_iota(jnp.int32, a.shape, 1)
    low, high = lane < k, lane >= HALF - k
    left_a, left_b = pltpu.roll(a, k, 1), pltpu.roll(b, k, 1)
    right_a, right_b = pltpu.roll(a, HALF - k, 1), pltpu.roll(b, HALF - k, 1)
    return (
        jnp.where(low, left_b, left_a) + jnp.where(high, right_b, right_a),
        jnp.where(low, left_a, left_b) + jnp.where(high, right_a, right_b),
    )


def advance(pairs, buffers, coef, trails):
    rows = pairs[0][0].shape[0]
    for step in range(STEPS):
        slots = [b.at[step % 2] for b in buffers]
        kept = slice(2 * step, 2 * step + 2)
        for slot, pair, trail in zip(slots, pairs, trails):
            for h in range(2):
                slot[h, PAD : PAD + rows] = pair[h]
                trail[0, h, kept] = slot[h, PAD + step : PAD + step + 2]
                trail[1, h, kept] = slot[h, PAD + rows - 2 - step : PAD + rows - step]
        after = []
        for slot, pair in zip(slots, pairs):
            sides = lane_sides(pair, 1)
            after.append(
                tuple(
                    coef[0, h] * pair[h]
                    + coef[1, h] * slot[h, PAD - 1 : PAD - 1 + rows]
                    + coef[2, h] * (slot[h, PAD + 1 : PAD + 1 + rows] + sides[h])
                    for h in range(2)
                )
            )
        pairs = after
    return pairs


def advance_windows(jobs, windows, buffers, coef_ref, trails):
    for step in range(STEPS):
        slots = [b.at[step % 2] for b in buffers]
        kept = slice(2 * step, 2 * step + 2)
        for (end, p), slot, window, trail in zip(jobs, slots, windows, trails):
            beside = PAD + 8 if end == 0 else PAD - 2
            for h in range(2):
                slot[h, PAD : PAD + 8] = window[h]
                slot[h, beside : beside + 2] = trail[end, h, kept]
        after = []
        for (end, p), slot in zip(jobs, slots):
            top = PAD if end == 0 else PAD - 2
            start = 1 + step if end == 0 else 7 - step
            center = tuple(slot[h, top + 1 : top + 9] for h in range(2))
            sides = lane_sides(center, 1)
            coef = coef_ref.at[end]
            after.append(
                tuple(
                    coef[0, h, start : start + 8] * center[h]
                    + coef[1, h, start : start + 8] * slot[h, top : top + 8]
                    + coef[2, h, start : start + 8] * (slot[h, top + 2 : top + 10] + sides[h])
                    for h in range(2)
                )
            )
        windows = after
    return windows


def radius_weights(radii_ref, rows):
    radii = [jnp.concatenate([radii_ref[f]] * (rows // 8), axis=0) for f in range(FIELDS)]
    return [
        [None, None] + [jnp.where(r >= float(k), 1.0, 0.0) for k in range(2, RADIUS + 1)]
        for r in radii
    ]


def row_total(likelihood_ref, start, rows, weights):
    def both(k):
        return (
            likelihood_ref[start - k : start - k + rows]
            + likelihood_ref[start + k : start + k + rows]
        )

    outer = both(RADIUS)
    for k in range(RADIUS - 1, 0, -1):
        outer = both(k) + weights[k + 1] * outer
    return likelihood_ref[start : start + rows] + outer


def column_total(totals, weights):
    score = tuple(sum((t[h] for t in totals[1:]), totals[0][h]) for h in range(2))
    mixed = score
    for k in range(1, RADIUS + 1):
        if k > 1:
            totals = [
                tuple(weights[f][k] * t for t in totals[f]) for f in range(FIELDS)
            ]
            mixed = tuple(sum((t[h] for t in totals[1:]), totals[0][h]) for h in range(2))
        sides = lane_sides(mixed, k)
        score = tuple(score[h] + sides[h] for h in range(2))
    return score


def local_statistics(scores, cells):
    def plus(terms):
        return sum(terms[1:], terms[0])

    peak = scores[0]
    for s in scores[1:]:
        peak = jnp.maximum(peak, s)
    importance = [jnp.exp(s - peak) for s in scores]
    total = plus(importance)
    inverse = 1.0 / total
    share = 1.0 / LOCAL
    center = [plus([c[f] for c in cells]) * share for f in range(FIELDS)]
    away = [[c[f] - center[f] for f in range(FIELDS)] for c in cells]
    drift = [
        plus([w * a[f] for w, a in zip(importance, away)]) * inverse for f in range(FIELDS)
    ]
    post, prior = [], []
    for i, j in pair_list:
        products = [a[i] * a[j] for a in away]
        prior.append(plus(products) * share)
        post.append(
            plus([w * p for w, p in zip(importance, products)]) * inverse - drift[i] * drift[j]
        )
    moved = [center[f] + drift[f] for f in range(FIELDS)]
    return [peak + jnp.log(total)] + moved + post + center + prior


def pack_kernel(
    radius_hbm, temper_hbm, fields_hbm, spread_hbm, flow_hbm, quantity_hbm, confidence_hbm,
    mask_hbm, last_ref, leading_ref, par_ref, tempering_ref, radii_ref,
    radius_ref, temper_ref, confidence_ref, mask_ref, sems,
):
    planes, rows = fields_hbm.shape[:2]
    tail = pl.ds(rows - HALO, HALO)
    head = pl.ds(0, HALO)
    sent = pl.ds(0, planes)
    pairs = (
        (confidence_hbm, confidence_ref),
        (mask_hbm, mask_ref),
        (spread_hbm, par_ref.at[0]),
        (flow_hbm, par_ref.at[1]),
        (quantity_hbm, par_ref.at[pl.ds(2, FIELDS)]),
        (temper_hbm, temper_ref),
        (radius_hbm, radius_ref),
        (fields_hbm.at[:, tail], last_ref.at[sent]),
        (fields_hbm.at[:, head], leading_ref.at[sent]),
    )
    copies = [
        pltpu.make_async_copy(source, target, sems.at[number])
        for number, (source, target) in enumerate(pairs)
    ]
    for copy in copies:
        copy.start()
    for copy in copies[:7]:
        copy.wait()
    for f in range(FIELDS):
        par_ref[5 + f] = -0.5 * mask_ref[f].astype(jnp.float32) * confidence_ref[f]
        radius = radius_ref[:, f : f + 1].astype(jnp.float32)
        radii_ref[f] = jnp.broadcast_to(radius, (8, HALF))
    for out_ref, part, first in ((last_ref, tail, rows - 4), (leading_ref, head, 0)):
        for p in range(2):
            out_ref[planes + p] = par_ref[p, part]
        for f in range(FIELDS):
            out_ref[planes + 2 + f, 0:4] = par_ref[2 + f, first : first + 4]
            out_ref[planes + 2 + f, 4:8] = par_ref[5 + f, first : first + 4]
    row = lax.broadcasted_iota(jnp.int32, (rows, rows), 0)
    column = lax.broadcasted_iota(jnp.int32, (rows, rows), 1)
    along = jnp.broadcast_to(temper_ref[...].astype(jnp.float32), (rows, rows))
    each = jnp.sum(jnp.where(row == column, along, 0.0), axis=1, keepdims=True)
    tempering_ref[...] = jnp.exp2(-jnp.broadcast_to(each, (rows, HALF)))
    for copy in copies[7:]:
        copy.wait()


def interior_kernel(
    own_ref, par_ref, temper_ref, radii_ref, field_ref, stats_ref, trail_ref,
    coef_ref, buffer_ref, likelihood_ref, score_ref,
):
    rows = own_ref.shape[1]
    inner = rows - 16
    spread, flow = split(par_ref[0]), split(par_ref[1])
    for h in range(2):
        coef_ref[0, h] = 1.0 - 4.0 * spread[h] - flow[h]
        coef_ref[1, h] = spread[h] + flow[h]
        coef_ref[2, h] = spread[h]
    weights = radius_weights(radii_ref, inner)

    def some_members(step, carry):
        first = step * TOGETHER
        planes = range(TOGETHER * FIELDS)
        pairs = advance(
            [split(own_ref[first * FIELDS + p]) for p in planes],
            [buffer_ref.at[p] for p in planes],
            coef_ref,
            [trail_ref.at[first * FIELDS + p] for p in planes],
        )
        for p in planes:
            f = p % FIELDS
            quantity, observed = split(par_ref[2 + f]), split(par_ref[5 + f])
            for h in range(2):
                field_ref[first + p // FIELDS, f, h] = pairs[p][h]
                misfit = pairs[p][h] - quantity[h]
                likelihood_ref[p, h] = observed[h] * misfit * misfit
        for u in range(TOGETHER):
            totals = [
                tuple(
                    row_total(likelihood_ref.at[u * FIELDS + f, h], 8, inner, weights[f])
                    for h in range(2)
                )
                for f in range(FIELDS)
            ]
            score = column_total(totals, weights)
            for h in range(2):
                score_ref[first + u, h] = temper_ref[8 : 8 + inner] * score[h]
        return carry

    lax.fori_loop(0, LOCAL // TOGETHER, some_members, 0)

    def one_group(g, carry):
        sub = pl.ds(pl.multiple_of(g * 8, 8), 8)
        deep = pl.ds(pl.multiple_of(g * 8 + 8, 8), 8)
        for h in range(2):
            scores = [score_ref[m, h, sub] for m in range(LOCAL)]
            cells = [[field_ref[m, f, h, deep] for f in range(FIELDS)] for m in range(LOCAL)]
            for number, value in enumerate(local_statistics(scores, cells)):
                stats_ref[g, number, :, h * HALF : (h + 1) * HALF] = value
        return carry

    lax.fori_loop(0, inner // 8, one_group, 0)


def edge_kernel(
    trail_ref, above_ref, below_ref, own_par_ref, temper_ref, radii_ref, inner_field_ref,
    inner_stats_ref, field_ref, stats_ref, coef_ref, buffer_ref, par_ref, wide_ref,
    likelihood_ref, score_ref,
):
    rows = own_par_ref.shape[1]
    ends = (slice(0, 8), slice(rows - 8, rows))
    halos = (above_ref, below_ref)
    base = FIELDS * LOCAL
    for g in range(rows // 8 - 2):
        stats_ref[1 + g] = inner_stats_ref[g]

    def framed(end, own, halo):
        return jnp.concatenate([halo, own] if end == 0 else [own, halo], axis=0)

    for end in range(2):
        spread = split(framed(end, own_par_ref[0, ends[end]], halos[end][base]))
        flow = split(framed(end, own_par_ref[1, ends[end]], halos[end][base + 1]))
        for h in range(2):
            coef_ref[end, 0, h] = 1.0 - 4.0 * spread[h] - flow[h]
            coef_ref[end, 1, h] = spread[h] + flow[h]
            coef_ref[end, 2, h] = spread[h]
    for p in range(6):
        half_plane = slice(0, 4) if p < FIELDS else slice(4, 8)
        for h in range(2):
            lane = slice(h * HALF, (h + 1) * HALF)
            par_ref[p, h, 4:8] = above_ref[base + 2 + p % FIELDS, half_plane, lane]
            par_ref[p, h, 8 : 8 + rows] = own_par_ref[2 + p, :, lane]
            par_ref[p, h, 8 + rows : 12 + rows] = below_ref[
                base + 2 + p % FIELDS, half_plane, lane
            ]
    weights = radius_weights(radii_ref, 8)

    def some_members(step, carry):
        first = step * TOGETHER
        jobs = [
            (end, p) for p in range(TOGETHER * FIELDS) for end in range(2)
        ]
        pairs = advance_windows(
            jobs,
            [split(halos[end][first * FIELDS + p]) for end, p in jobs],
            [buffer_ref.at[end, p] for end, p in jobs],
            coef_ref,
            [trail_ref.at[first * FIELDS + p] for end, p in jobs],
        )
        for (end, p), pair in zip(jobs, pairs):
            m, f = first + p // FIELDS, p % FIELDS
            start = (4, rows - 4)[end]
            for h in range(2):
                wide = wide_ref.at[end, p, h]
                new = pair[h]
                old = inner_field_ref[m, f, h, (4, rows - 12)[end] : (12, rows - 4)[end]]
                wide[0:8] = (new, old)[end]
                wide[8:16] = (old, new)[end]
                field_ref[m, f, end, h] = wide[4:12]
                misfit = framed(end, old, new) - par_ref[f, h, start : start + 16]
                observed = par_ref[3 + f, h, start : start + 16]
                likelihood_ref[end, p, h] = observed * misfit * misfit
        for u in range(TOGETHER):
            for end in range(2):
                totals = [
                    tuple(
                        row_total(
                            likelihood_ref.at[end, u * FIELDS + f, h], 4, 8, weights[f]
                        )
                        for h in range(2)
                    )
                    for f in range(FIELDS)
                ]
                score = column_total(totals, weights)
                for h in range(2):
                    score_ref[first + u, end, h] = temper_ref[ends[end]] * score[h]
        return carry

    lax.fori_loop(0, LOCAL // TOGETHER, some_members, 0)

    def one_half(h, carry):
        lane = pl.ds(pl.multiple_of(h * HALF, HALF), HALF)
        for end in range(2):
            scores = [score_ref[m, end, h] for m in range(LOCAL)]
            cells = [[field_ref[m, f, end, h] for f in range(FIELDS)] for m in range(LOCAL)]
            for number, value in enumerate(local_statistics(scores, cells)):
                stats_ref[(0, rows // 8 - 1)[end], number, :, lane] = value
        return carry

    lax.fori_loop(0, 2, one_half, 0)


def merged(parts, add, biggest):
    peak = biggest(parts[0])
    mass = [jnp.exp(p - peak) for p in parts[0]]
    total = add(mass)
    out = [peak + jnp.log(total)]
    for first, weights in ((1, mass), (10, None)):
        count = len(mass)

        def average(terms):
            if weights is None:
                return add(terms)
            return add([weights[s] * terms[s] for s in range(count)])

        share = 1.0 / (total if weights is not None else add([jnp.ones_like(m) for m in mass]))
        means = [average(parts[first + f]) * share for f in range(FIELDS)]
        away = [[parts[first + f][s] - means[f] for s in range(count)] for f in range(FIELDS)]
        out += means
        for number, (i, j) in enumerate(pair_list):
            second = parts[first + FIELDS + number]
            out.append(
                average([second[s] + away[i][s] * away[j][s] for s in range(count)]) * share
            )
    return out


def merge_x_kernel(part_ref, out_ref):
    def add(terms):
        return sum(terms[1:], terms[0])

    def biggest(terms):
        peak = terms[0]
        for t in terms[1:]:
            peak = jnp.maximum(peak, t)
        return peak

    for half in range(2):
        lane = pl.ds(half * 128, 128)
        parts = [[part_ref[s, p, :, lane] for s in range(X)] for p in range(STATS)]
        out = merged(parts, add, biggest)
        for p in range(STATS):
            out_ref[pl.ds(half * 8 * STATS + p, 8, stride=STATS), :] = out[p]


def merge_z_kernel(part_ref, out_ref):
    sources = part_ref.shape[0] // STATS
    blocks = sources // 8

    def add(terms):
        return jnp.sum(sum(terms[1:], terms[0]), axis=0, keepdims=True)

    def biggest(terms):
        peak = terms[0]
        for t in terms[1:]:
            peak = jnp.maximum(peak, t)
        return jnp.max(peak, axis=0, keepdims=True)

    parts = [
        [part_ref[pl.ds(b * 8 * STATS + p, 8, stride=STATS), :] for b in range(blocks)]
        for p in range(STATS)
    ]
    out = merged(parts, add, biggest)
    diagonal = (0, 2, 5)
    post_cov = [out[4 + n] + (jitter if n in diagonal else 0.0) for n in range(6)]
    prior_cov = [out[13 + n] + (jitter if n in diagonal else 0.0) for n in range(6)]
    gain = lower_product(cholesky_rows(post_cov), lower_inverse(cholesky_rows(prior_cov)))
    result = list(gain)
    for row in range(FIELDS):
        running = out[1 + row]
        for source in range(row + 1):
            running = running - gain[row * (row + 1) // 2 + source] * out[10 + source]
        result.append(running)
    for p in range(COEFS):
        value = jnp.broadcast_to(result[p], (8, 128))
        for b in range(blocks):
            out_ref[pl.ds(b * 8 * COEFS + p, 8, stride=COEFS), :] = value


def spread_kernel(coef_ref, out_ref):
    for half in range(2):
        lane = pl.ds(half * HALF, HALF)
        for p in range(COEFS):
            value = coef_ref[pl.ds(half * 8 * COEFS + p, 8, stride=COEFS), :]
            for target in range(X):
                out_ref[target, p, :, lane] = value


def apply_kernel(coef_ref, inner_ref, edge_ref, out_ref):
    last = X - 1

    def one_member(m, carry):
        for g in range(X):
            for h in range(2):
                lane = slice(h * HALF, (h + 1) * HALF)
                if g in (0, last):
                    cells = [edge_ref[m, f, 0 if g == 0 else 1, h] for f in range(FIELDS)]
                else:
                    cells = [inner_ref[m, f, h, g * 8 : g * 8 + 8] for f in range(FIELDS)]
                for row in range(FIELDS):
                    running = coef_ref[g, 6 + row, :, lane]
                    for source in range(row + 1):
                        entry = coef_ref[g, row * (row + 1) // 2 + source, :, lane]
                        running = running + entry * cells[source]
                    out_ref[m, row, g * 8 : g * 8 + 8, lane] = running
        return carry

    lax.fori_loop(0, LOCAL, one_member, 0)


def f32(*shape):
    return jax.ShapeDtypeStruct(shape, jnp.float32)


def body(
    sample_group,
    spreading_ratio,
    flow_ratio,
    measured_quantity,
    measured_confidence,
    obs_mask,
    radius,
    temper,
):
    rows, cols = sample_group.shape[2:]
    z = lax.axis_size("z")
    sent = LOCAL * FIELDS + 2 + FIELDS
    planes = sample_group.reshape(LOCAL * FIELDS, rows, cols)
    last, leading, own_par, tempering, radii = pl.pallas_call(
        pack_kernel,
        out_shape=(
            f32(sent, HALO, cols),
            f32(sent, HALO, cols),
            f32(MOVING, rows, cols),
            f32(rows, HALF),
            f32(FIELDS, 8, HALF),
        ),
        in_specs=[HBM] * 8,
        out_specs=(VMEM,) * 5,
        scratch_shapes=[
            pltpu.VMEM((1, FIELDS), jnp.int32),
            pltpu.VMEM((1, rows), jnp.int32),
            pltpu.VMEM((FIELDS, rows, cols), jnp.float32),
            pltpu.VMEM((FIELDS, rows, cols), jnp.int32),
            pltpu.SemaphoreType.DMA((9,)),
        ],
        compiler_params=LARGE,
        name="pack",
    )(
        *(
            pltpu.with_memory_space_constraint(array, pltpu.HBM)
            for array in (
                radius.reshape(1, FIELDS),
                temper.reshape(1, rows),
                planes,
                spreading_ratio,
                flow_ratio,
                measured_quantity,
                measured_confidence,
                obs_mask,
            )
        )
    )
    count = lax.axis_size("space")
    up = [(i, (i + 1) % count) for i in range(count)]
    down = [(j, i) for i, j in up]
    above = lax.ppermute(last, "space", up)
    below = lax.ppermute(leading, "space", down)
    inner_field, inner_stats, trail = pl.pallas_call(
        interior_kernel,
        out_shape=(
            f32(LOCAL, FIELDS, 2, rows, HALF),
            f32(rows // 8 - 2, STATS, 8, cols),
            f32(LOCAL * FIELDS, 2, 2, 2 * STEPS, HALF),
        ),
        in_specs=[VMEM] * 4,
        out_specs=(VMEM,) * 3,
        scratch_shapes=[
            pltpu.VMEM((3, 2, rows, HALF), jnp.float32),
            pltpu.VMEM((TOGETHER * FIELDS, 2, 2, rows + 2 * PAD, HALF), jnp.float32),
            pltpu.VMEM((TOGETHER * FIELDS, 2, rows, HALF), jnp.float32),
            pltpu.VMEM((LOCAL, 2, rows - 16, HALF), jnp.float32),
        ],
        compiler_params=LARGE,
        name="interior",
    )(planes, own_par, tempering, radii)

    edge_field, stats = pl.pallas_call(
        edge_kernel,
        out_shape=(f32(LOCAL, FIELDS, 2, 2, 8, HALF), f32(X, STATS, 8, cols)),
        in_specs=[VMEM] * 8,
        out_specs=(VMEM, VMEM),
        scratch_shapes=[
            pltpu.VMEM((2, 3, 2, 16, HALF), jnp.float32),
            pltpu.VMEM((2, TOGETHER * FIELDS, 2, 2, 8 + 2 * PAD, HALF), jnp.float32),
            pltpu.VMEM((6, 2, rows + 16, HALF), jnp.float32),
            pltpu.VMEM((2, TOGETHER * FIELDS, 2, 16, HALF), jnp.float32),
            pltpu.VMEM((2, TOGETHER * FIELDS, 2, 16, HALF), jnp.float32),
            pltpu.VMEM((LOCAL, 2, 2, 8, HALF), jnp.float32),
        ],
        compiler_params=LARGE,
        name="edge",
    )(trail, above, below, own_par, tempering, radii, inner_field, inner_stats)

    stats = lax.all_to_all(stats, "x", 0, 0, tiled=True)
    stats = pl.pallas_call(
        merge_x_kernel,
        out_shape=f32(z * STATS, 128),
        in_specs=[VMEM],
        out_specs=VMEM,
        compiler_params=SMALL,
        name="merge_x",
    )(stats)
    stats = lax.all_to_all(stats.reshape(z, STATS, 1, 128), "z", 0, 0, tiled=True)
    coef = pl.pallas_call(
        merge_z_kernel,
        out_shape=f32(z * COEFS, 128),
        in_specs=[VMEM],
        out_specs=VMEM,
        compiler_params=SMALL,
        name="merge_z",
    )(stats.reshape(z * STATS, 128))
    coef = lax.all_to_all(coef.reshape(z, COEFS, 1, 128), "z", 0, 0, tiled=True)
    coef = pl.pallas_call(
        spread_kernel,
        out_shape=f32(X, COEFS, 8, cols),
        in_specs=[VMEM],
        out_specs=VMEM,
        compiler_params=SMALL,
        name="spread",
    )(coef.reshape(z * COEFS, 128))
    coef = lax.all_to_all(coef, "x", 0, 0, tiled=True)
    return pl.pallas_call(
        apply_kernel,
        out_shape=f32(LOCAL, FIELDS, rows, cols),
        in_specs=[VMEM] * 3,
        out_specs=VMEM,
        compiler_params=LARGE,
        name="apply",
    )(coef, inner_field, edge_field)


def solution(mesh):
    devices = mesh.devices
    fine = Mesh(devices.reshape(devices.shape[0] // X, X, devices.shape[1]), ("z", "x", "space"))
    member = ("z", "x")
    in_specs = (
        P(member, None, "space", None),
        P("space", None),
        P("space", None),
        P(None, "space", None),
        P(None, "space", None),
        P(None, "space", None),
        P(),
        P("space"),
    )
    out_specs = P(member, None, "space", None)
    return jax.shard_map(body, mesh=fine, in_specs=in_specs, out_specs=out_specs, check_vma=False)
```

```python
import jax
import jax.numpy as jnp
from jax import lax
from jax.experimental import pallas as pl
from jax.experimental.pallas import tpu as pltpu
from jax.sharding import Mesh, PartitionSpec as P

STEPS = 4
RADIUS = 4
LOCAL = 8
FIELDS = 3
X = 4
HALO = 8
STATS = 19
COEFS = 9

jitter = 0.05
pair_list = ((0, 0), (1, 0), (1, 1), (2, 0), (2, 1), (2, 2))
VMEM = pl.BlockSpec(memory_space=pltpu.VMEM)
HBM = pl.BlockSpec(memory_space=pltpu.HBM)

LARGE = pltpu.CompilerParams(vmem_limit_bytes=8 << 20)
SMALL = pltpu.CompilerParams(vmem_limit_bytes=2 << 20)


def cholesky_rows(matrix):
    first = jnp.sqrt(matrix[0])
    second = matrix[1] / first
    fourth = matrix[3] / first
    third = jnp.sqrt(matrix[2] - second * second)
    fifth = (matrix[4] - fourth * second) / third
    sixth = jnp.sqrt(matrix[5] - fourth * fourth - fifth * fifth)
    return [first, second, third, fourth, fifth, sixth]


def lower_inverse(packed):
    head = 1.0 / packed[0]
    middle = 1.0 / packed[2]
    tail = 1.0 / packed[5]
    below_head = -packed[1] * head * middle
    below_middle = -packed[4] * middle * tail
    corner = -(packed[3] * head + packed[4] * below_head) * tail
    return [head, below_head, middle, corner, below_middle, tail]


def lower_product(left_side, right_side):
    return [
        left_side[0] * right_side[0],
        left_side[1] * right_side[0] + left_side[2] * right_side[1],
        left_side[2] * right_side[2],
        left_side[3] * right_side[0] + left_side[4] * right_side[1] + left_side[5] * right_side[3],
        left_side[4] * right_side[2] + left_side[5] * right_side[4],
        left_side[5] * right_side[5],
    ]


HALF = 128
PAD = 8
TOGETHER = 8
MOVING = 8


def split(value):
    return value[:, :HALF], value[:, HALF:]


def lane_sides(pair, k):
    a, b = pair
    lane = lax.broadcasted_iota(jnp.int32, a.shape, 1)
    low, high = lane < k, lane >= HALF - k
    left_a, left_b = pltpu.roll(a, k, 1), pltpu.roll(b, k, 1)
    right_a, right_b = pltpu.roll(a, HALF - k, 1), pltpu.roll(b, HALF - k, 1)
    return (
        jnp.where(low, left_b, left_a) + jnp.where(high, right_b, right_a),
        jnp.where(low, left_a, left_b) + jnp.where(high, right_a, right_b),
    )


def advance(pairs, buffers, coef, trails):
    rows = pairs[0][0].shape[0]
    for step in range(STEPS):
        slots = [b.at[step % 2] for b in buffers]
        kept = slice(2 * step, 2 * step + 2)
        for slot, pair, trail in zip(slots, pairs, trails):
            for h in range(2):
                slot[h, PAD : PAD + rows] = pair[h]
                trail[0, h, kept] = slot[h, PAD + step : PAD + step + 2]
                trail[1, h, kept] = slot[h, PAD + rows - 2 - step : PAD + rows - step]
        after = []
        for slot, pair in zip(slots, pairs):
            sides = lane_sides(pair, 1)
            after.append(
                tuple(
                    coef[0, h] * pair[h]
                    + coef[1, h] * slot[h, PAD - 1 : PAD - 1 + rows]
                    + coef[2, h] * (slot[h, PAD + 1 : PAD + 1 + rows] + sides[h])
                    for h in range(2)
                )
            )
        pairs = after
    return pairs


def advance_windows(jobs, windows, buffers, coef_ref, trails):
    for step in range(STEPS):
        slots = [b.at[step % 2] for b in buffers]
        kept = slice(2 * step, 2 * step + 2)
        for (end, p), slot, window, trail in zip(jobs, slots, windows, trails):
            beside = PAD + 8 if end == 0 else PAD - 2
            for h in range(2):
                slot[h, PAD : PAD + 8] = window[h]
                slot[h, beside : beside + 2] = trail[end, h, kept]
        after = []
        for (end, p), slot in zip(jobs, slots):
            top = PAD if end == 0 else PAD - 2
            start = 1 + step if end == 0 else 7 - step
            center = tuple(slot[h, top + 1 : top + 9] for h in range(2))
            sides = lane_sides(center, 1)
            coef = coef_ref.at[end]
            after.append(
                tuple(
                    coef[0, h, start : start + 8] * center[h]
                    + coef[1, h, start : start + 8] * slot[h, top : top + 8]
                    + coef[2, h, start : start + 8] * (slot[h, top + 2 : top + 10] + sides[h])
                    for h in range(2)
                )
            )
        windows = after
    return windows


def radius_weights(radii_ref, rows):
    radii = [jnp.concatenate([radii_ref[f]] * (rows // 8), axis=0) for f in range(FIELDS)]
    return [
        [None, None] + [jnp.where(r >= float(k), 1.0, 0.0) for k in range(2, RADIUS + 1)]
        for r in radii
    ]


def row_total(likelihood_ref, start, rows, weights):
    def both(k):
        return (
            likelihood_ref[start - k : start - k + rows]
            + likelihood_ref[start + k : start + k + rows]
        )

    outer = both(RADIUS)
    for k in range(RADIUS - 1, 0, -1):
        outer = both(k) + weights[k + 1] * outer
    return likelihood_ref[start : start + rows] + outer


def column_total(totals, weights):
    score = tuple(sum((t[h] for t in totals[1:]), totals[0][h]) for h in range(2))
    mixed = score
    for k in range(1, RADIUS + 1):
        if k > 1:
            totals = [
                tuple(weights[f][k] * t for t in totals[f]) for f in range(FIELDS)
            ]
            mixed = tuple(sum((t[h] for t in totals[1:]), totals[0][h]) for h in range(2))
        sides = lane_sides(mixed, k)
        score = tuple(score[h] + sides[h] for h in range(2))
    return score


def local_statistics(scores, cells):
    def plus(terms):
        return sum(terms[1:], terms[0])

    peak = scores[0]
    for s in scores[1:]:
        peak = jnp.maximum(peak, s)
    importance = [jnp.exp(s - peak) for s in scores]
    total = plus(importance)
    inverse = 1.0 / total
    share = 1.0 / LOCAL
    center = [plus([c[f] for c in cells]) * share for f in range(FIELDS)]
    away = [[c[f] - center[f] for f in range(FIELDS)] for c in cells]
    drift = [
        plus([w * a[f] for w, a in zip(importance, away)]) * inverse for f in range(FIELDS)
    ]
    post, prior = [], []
    for i, j in pair_list:
        products = [a[i] * a[j] for a in away]
        prior.append(plus(products) * share)
        post.append(
            plus([w * p for w, p in zip(importance, products)]) * inverse - drift[i] * drift[j]
        )
    moved = [center[f] + drift[f] for f in range(FIELDS)]
    return [peak + jnp.log(total)] + moved + post + center + prior


def is_odd():
    return lax.rem(lax.axis_index("space"), 2) == 1


def pack_kernel(
    radius_hbm, temper_hbm, fields_hbm, spread_hbm, flow_hbm, quantity_hbm, confidence_hbm,
    mask_hbm, far_ref, near_ref, par_ref, tempering_ref, radii_ref,
    radius_ref, temper_ref, confidence_ref, mask_ref, sems,
):
    planes, rows = fields_hbm.shape[:2]
    odd = is_odd()
    top = jnp.where(odd, rows - HALO, 0)
    far = pl.ds(pl.multiple_of(top, 8), HALO)
    near = pl.ds(pl.multiple_of(rows - HALO - top, 8), HALO)
    sent = pl.ds(0, planes)
    pairs = (
        (confidence_hbm, confidence_ref),
        (mask_hbm, mask_ref),
        (spread_hbm, par_ref.at[0]),
        (flow_hbm, par_ref.at[1]),
        (quantity_hbm, par_ref.at[pl.ds(2, FIELDS)]),
        (temper_hbm, temper_ref),
        (radius_hbm, radius_ref),
        (fields_hbm.at[:, far], far_ref.at[sent]),
        (fields_hbm.at[:, near], near_ref.at[sent]),
    )
    copies = [
        pltpu.make_async_copy(source, target, sems.at[number])
        for number, (source, target) in enumerate(pairs)
    ]
    for copy in copies:
        copy.start()
    for copy in copies[:7]:
        copy.wait()
    for f in range(FIELDS):
        par_ref[5 + f] = -0.5 * mask_ref[f].astype(jnp.float32) * confidence_ref[f]
        radius = radius_ref[:, f : f + 1].astype(jnp.float32)
        radii_ref[f] = jnp.broadcast_to(radius, (8, HALF))
    def facing(plane, count):
        tail, head = par_ref[plane, rows - count : rows], par_ref[plane, 0:count]
        return jnp.where(odd, tail, head), jnp.where(odd, head, tail)

    for p in range(2):
        far_ref[planes + p], near_ref[planes + p] = facing(p, HALO)
    for f in range(FIELDS):
        for source, part in ((2 + f, slice(0, 4)), (5 + f, slice(4, 8))):
            far_ref[planes + 2 + f, part], near_ref[planes + 2 + f, part] = facing(source, 4)
    row = lax.broadcasted_iota(jnp.int32, (rows, rows), 0)
    column = lax.broadcasted_iota(jnp.int32, (rows, rows), 1)
    along = jnp.broadcast_to(temper_ref[...].astype(jnp.float32), (rows, rows))
    each = jnp.sum(jnp.where(row == column, along, 0.0), axis=1, keepdims=True)
    tempering_ref[...] = jnp.exp2(-jnp.broadcast_to(each, (rows, HALF)))
    for copy in copies[7:]:
        copy.wait()


def interior_kernel(
    own_ref, par_ref, temper_ref, radii_ref, field_ref, stats_ref, trail_ref,
    coef_ref, buffer_ref, likelihood_ref, score_ref,
):
    rows = own_ref.shape[1]
    inner = rows - 16
    spread, flow = split(par_ref[0]), split(par_ref[1])
    for h in range(2):
        coef_ref[0, h] = 1.0 - 4.0 * spread[h] - flow[h]
        coef_ref[1, h] = spread[h] + flow[h]
        coef_ref[2, h] = spread[h]
    weights = radius_weights(radii_ref, inner)

    def some_members(step, carry):
        first = step * TOGETHER
        planes = range(TOGETHER * FIELDS)
        pairs = advance(
            [split(own_ref[first * FIELDS + p]) for p in planes],
            [buffer_ref.at[p] for p in planes],
            coef_ref,
            [trail_ref.at[first * FIELDS + p] for p in planes],
        )
        for p in planes:
            f = p % FIELDS
            quantity, observed = split(par_ref[2 + f]), split(par_ref[5 + f])
            for h in range(2):
                field_ref[first + p // FIELDS, f, h] = pairs[p][h]
                misfit = pairs[p][h] - quantity[h]
                likelihood_ref[p, h] = observed[h] * misfit * misfit
        for u in range(TOGETHER):
            totals = [
                tuple(
                    row_total(likelihood_ref.at[u * FIELDS + f, h], 8, inner, weights[f])
                    for h in range(2)
                )
                for f in range(FIELDS)
            ]
            score = column_total(totals, weights)
            for h in range(2):
                score_ref[first + u, h] = temper_ref[8 : 8 + inner] * score[h]
        return carry

    lax.fori_loop(0, LOCAL // TOGETHER, some_members, 0)

    def one_group(g, carry):
        sub = pl.ds(pl.multiple_of(g * 8, 8), 8)
        deep = pl.ds(pl.multiple_of(g * 8 + 8, 8), 8)
        for h in range(2):
            scores = [score_ref[m, h, sub] for m in range(LOCAL)]
            cells = [[field_ref[m, f, h, deep] for f in range(FIELDS)] for m in range(LOCAL)]
            for number, value in enumerate(local_statistics(scores, cells)):
                stats_ref[g, number, :, h * HALF : (h + 1) * HALF] = value
        return carry

    lax.fori_loop(0, inner // 8, one_group, 0)


def edge_kernel(
    trail_ref, far_ref, near_ref, own_par_ref, temper_ref, radii_ref, inner_field_ref,
    inner_stats_ref, field_ref, stats_ref, halo_ref, coef_ref, buffer_ref, par_ref, wide_ref,
    likelihood_ref, score_ref,
):
    rows = own_par_ref.shape[1]
    ends = (slice(0, 8), slice(rows - 8, rows))
    odd = is_odd()
    for plane in range(far_ref.shape[0]):
        far, near = far_ref[plane], near_ref[plane]
        halo_ref[0, plane] = jnp.where(odd, near, far)
        halo_ref[1, plane] = jnp.where(odd, far, near)
    above_ref, below_ref = halos = (halo_ref.at[0], halo_ref.at[1])
    base = FIELDS * LOCAL
    for g in range(rows // 8 - 2):
        stats_ref[1 + g] = inner_stats_ref[g]

    def framed(end, own, halo):
        return jnp.concatenate([halo, own] if end == 0 else [own, halo], axis=0)

    for end in range(2):
        spread = split(framed(end, own_par_ref[0, ends[end]], halos[end][base]))
        flow = split(framed(end, own_par_ref[1, ends[end]], halos[end][base + 1]))
        for h in range(2):
            coef_ref[end, 0, h] = 1.0 - 4.0 * spread[h] - flow[h]
            coef_ref[end, 1, h] = spread[h] + flow[h]
            coef_ref[end, 2, h] = spread[h]
    for p in range(6):
        half_plane = slice(0, 4) if p < FIELDS else slice(4, 8)
        for h in range(2):
            lane = slice(h * HALF, (h + 1) * HALF)
            par_ref[p, h, 4:8] = above_ref[base + 2 + p % FIELDS, half_plane, lane]
            par_ref[p, h, 8 : 8 + rows] = own_par_ref[2 + p, :, lane]
            par_ref[p, h, 8 + rows : 12 + rows] = below_ref[
                base + 2 + p % FIELDS, half_plane, lane
            ]
    weights = radius_weights(radii_ref, 8)

    def some_members(step, carry):
        first = step * TOGETHER
        jobs = [
            (end, p) for p in range(TOGETHER * FIELDS) for end in range(2)
        ]
        pairs = advance_windows(
            jobs,
            [split(halos[end][first * FIELDS + p]) for end, p in jobs],
            [buffer_ref.at[end, p] for end, p in jobs],
            coef_ref,
            [trail_ref.at[first * FIELDS + p] for end, p in jobs],
        )
        for (end, p), pair in zip(jobs, pairs):
            m, f = first + p // FIELDS, p % FIELDS
            start = (4, rows - 4)[end]
            for h in range(2):
                wide = wide_ref.at[end, p, h]
                new = pair[h]
                old = inner_field_ref[m, f, h, (4, rows - 12)[end] : (12, rows - 4)[end]]
                wide[0:8] = (new, old)[end]
                wide[8:16] = (old, new)[end]
                field_ref[m, f, end, h] = wide[4:12]
                misfit = framed(end, old, new) - par_ref[f, h, start : start + 16]
                observed = par_ref[3 + f, h, start : start + 16]
                likelihood_ref[end, p, h] = observed * misfit * misfit
        for u in range(TOGETHER):
            for end in range(2):
                totals = [
                    tuple(
                        row_total(
                            likelihood_ref.at[end, u * FIELDS + f, h], 4, 8, weights[f]
                        )
                        for h in range(2)
                    )
                    for f in range(FIELDS)
                ]
                score = column_total(totals, weights)
                for h in range(2):
                    score_ref[first + u, end, h] = temper_ref[ends[end]] * score[h]
        return carry

    lax.fori_loop(0, LOCAL // TOGETHER, some_members, 0)

    def one_half(h, carry):
        lane = pl.ds(pl.multiple_of(h * HALF, HALF), HALF)
        for end in range(2):
            scores = [score_ref[m, end, h] for m in range(LOCAL)]
            cells = [[field_ref[m, f, end, h] for f in range(FIELDS)] for m in range(LOCAL)]
            for number, value in enumerate(local_statistics(scores, cells)):
                stats_ref[(0, rows // 8 - 1)[end], number, :, lane] = value
        return carry

    lax.fori_loop(0, 2, one_half, 0)


def merged(parts, add, biggest):
    peak = biggest(parts[0])
    mass = [jnp.exp(p - peak) for p in parts[0]]
    total = add(mass)
    out = [peak + jnp.log(total)]
    for first, weights in ((1, mass), (10, None)):
        count = len(mass)

        def average(terms):
            if weights is None:
                return add(terms)
            return add([weights[s] * terms[s] for s in range(count)])

        share = 1.0 / (total if weights is not None else add([jnp.ones_like(m) for m in mass]))
        means = [average(parts[first + f]) * share for f in range(FIELDS)]
        away = [[parts[first + f][s] - means[f] for s in range(count)] for f in range(FIELDS)]
        out += means
        for number, (i, j) in enumerate(pair_list):
            second = parts[first + FIELDS + number]
            out.append(
                average([second[s] + away[i][s] * away[j][s] for s in range(count)]) * share
            )
    return out


def merge_x_kernel(part_ref, out_ref):
    def add(terms):
        return sum(terms[1:], terms[0])

    def biggest(terms):
        peak = terms[0]
        for t in terms[1:]:
            peak = jnp.maximum(peak, t)
        return peak

    for half in range(2):
        lane = pl.ds(half * 128, 128)
        parts = [[part_ref[s, p, :, lane] for s in range(X)] for p in range(STATS)]
        out = merged(parts, add, biggest)
        for p in range(STATS):
            out_ref[pl.ds(half * 8 * STATS + p, 8, stride=STATS), :] = out[p]


def merge_z_kernel(part_ref, out_ref):
    sources = part_ref.shape[0] // STATS
    blocks = sources // 8

    def add(terms):
        return jnp.sum(sum(terms[1:], terms[0]), axis=0, keepdims=True)

    def biggest(terms):
        peak = terms[0]
        for t in terms[1:]:
            peak = jnp.maximum(peak, t)
        return jnp.max(peak, axis=0, keepdims=True)

    parts = [
        [part_ref[pl.ds(b * 8 * STATS + p, 8, stride=STATS), :] for b in range(blocks)]
        for p in range(STATS)
    ]
    out = merged(parts, add, biggest)
    diagonal = (0, 2, 5)
    post_cov = [out[4 + n] + (jitter if n in diagonal else 0.0) for n in range(6)]
    prior_cov = [out[13 + n] + (jitter if n in diagonal else 0.0) for n in range(6)]
    gain = lower_product(cholesky_rows(post_cov), lower_inverse(cholesky_rows(prior_cov)))
    result = list(gain)
    for row in range(FIELDS):
        running = out[1 + row]
        for source in range(row + 1):
            running = running - gain[row * (row + 1) // 2 + source] * out[10 + source]
        result.append(running)
    for p in range(COEFS):
        value = jnp.broadcast_to(result[p], (8, 128))
        for b in range(blocks):
            out_ref[pl.ds(b * 8 * COEFS + p, 8, stride=COEFS), :] = value


def spread_kernel(coef_ref, out_ref):
    for half in range(2):
        lane = pl.ds(half * HALF, HALF)
        for p in range(COEFS):
            value = coef_ref[pl.ds(half * 8 * COEFS + p, 8, stride=COEFS), :]
            for target in range(X):
                out_ref[target, p, :, lane] = value


def apply_kernel(coef_ref, inner_ref, edge_ref, out_ref):
    last = X - 1

    def one_member(m, carry):
        for g in range(X):
            for h in range(2):
                lane = slice(h * HALF, (h + 1) * HALF)
                if g in (0, last):
                    cells = [edge_ref[m, f, 0 if g == 0 else 1, h] for f in range(FIELDS)]
                else:
                    cells = [inner_ref[m, f, h, g * 8 : g * 8 + 8] for f in range(FIELDS)]
                for row in range(FIELDS):
                    running = coef_ref[g, 6 + row, :, lane]
                    for source in range(row + 1):
                        entry = coef_ref[g, row * (row + 1) // 2 + source, :, lane]
                        running = running + entry * cells[source]
                    out_ref[m, row, g * 8 : g * 8 + 8, lane] = running
        return carry

    lax.fori_loop(0, LOCAL, one_member, 0)


def f32(*shape):
    return jax.ShapeDtypeStruct(shape, jnp.float32)


def body(
    sample_group,
    spreading_ratio,
    flow_ratio,
    measured_quantity,
    measured_confidence,
    obs_mask,
    radius,
    temper,
):
    rows, cols = sample_group.shape[2:]
    z = lax.axis_size("z")
    sent = LOCAL * FIELDS + 2 + FIELDS
    planes = sample_group.reshape(LOCAL * FIELDS, rows, cols)
    far, near, own_par, tempering, radii = pl.pallas_call(
        pack_kernel,
        out_shape=(
            f32(sent, HALO, cols),
            f32(sent, HALO, cols),
            f32(MOVING, rows, cols),
            f32(rows, HALF),
            f32(FIELDS, 8, HALF),
        ),
        in_specs=[HBM] * 8,
        out_specs=(VMEM,) * 5,
        scratch_shapes=[
            pltpu.VMEM((1, FIELDS), jnp.int32),
            pltpu.VMEM((1, rows), jnp.int32),
            pltpu.VMEM((FIELDS, rows, cols), jnp.float32),
            pltpu.VMEM((FIELDS, rows, cols), jnp.int32),
            pltpu.SemaphoreType.DMA((9,)),
        ],
        compiler_params=LARGE,
        name="pack",
    )(
        *(
            pltpu.with_memory_space_constraint(array, pltpu.HBM)
            for array in (
                radius.reshape(1, FIELDS),
                temper.reshape(1, rows),
                planes,
                spreading_ratio,
                flow_ratio,
                measured_quantity,
                measured_confidence,
                obs_mask,
            )
        )
    )
    count = lax.axis_size("space")
    between = [(i, (i + 1 if i % 2 else i - 1) % count) for i in range(count)]
    inside = [(i, (i - 1 if i % 2 else i + 1) % count) for i in range(count)]
    far = lax.ppermute(far, "space", between)
    near = lax.ppermute(near, "space", inside)

    inner_field, inner_stats, trail = pl.pallas_call(
        interior_kernel,
        out_shape=(
            f32(LOCAL, FIELDS, 2, rows, HALF),
            f32(rows // 8 - 2, STATS, 8, cols),
            f32(LOCAL * FIELDS, 2, 2, 2 * STEPS, HALF),
        ),
        in_specs=[VMEM] * 4,
        out_specs=(VMEM,) * 3,
        scratch_shapes=[
            pltpu.VMEM((3, 2, rows, HALF), jnp.float32),
            pltpu.VMEM((TOGETHER * FIELDS, 2, 2, rows + 2 * PAD, HALF), jnp.float32),
            pltpu.VMEM((TOGETHER * FIELDS, 2, rows, HALF), jnp.float32),
            pltpu.VMEM((LOCAL, 2, rows - 16, HALF), jnp.float32),
        ],
        compiler_params=LARGE,
        name="interior",
    )(planes, own_par, tempering, radii)

    edge_field, stats = pl.pallas_call(
        edge_kernel,
        out_shape=(f32(LOCAL, FIELDS, 2, 2, 8, HALF), f32(X, STATS, 8, cols)),
        in_specs=[VMEM] * 8,
        out_specs=(VMEM, VMEM),
        scratch_shapes=[
            pltpu.VMEM((2, sent, HALO, cols), jnp.float32),
            pltpu.VMEM((2, 3, 2, 16, HALF), jnp.float32),
            pltpu.VMEM((2, TOGETHER * FIELDS, 2, 2, 8 + 2 * PAD, HALF), jnp.float32),
            pltpu.VMEM((6, 2, rows + 16, HALF), jnp.float32),
            pltpu.VMEM((2, TOGETHER * FIELDS, 2, 16, HALF), jnp.float32),
            pltpu.VMEM((2, TOGETHER * FIELDS, 2, 16, HALF), jnp.float32),
            pltpu.VMEM((LOCAL, 2, 2, 8, HALF), jnp.float32),
        ],
        compiler_params=LARGE,
        name="edge",
    )(trail, far, near, own_par, tempering, radii, inner_field, inner_stats)

    stats = lax.all_to_all(stats, "x", 0, 0, tiled=True)
    stats = pl.pallas_call(
        merge_x_kernel,
        out_shape=f32(z * STATS, 128),
        in_specs=[VMEM],
        out_specs=VMEM,
        compiler_params=SMALL,
        name="merge_x",
    )(stats)
    stats = lax.all_to_all(stats.reshape(z, STATS, 1, 128), "z", 0, 0, tiled=True)
    coef = pl.pallas_call(
        merge_z_kernel,
        out_shape=f32(z * COEFS, 128),
        in_specs=[VMEM],
        out_specs=VMEM,
        compiler_params=SMALL,
        name="merge_z",
    )(stats.reshape(z * STATS, 128))
    coef = lax.all_to_all(coef.reshape(z, COEFS, 1, 128), "z", 0, 0, tiled=True)
    coef = pl.pallas_call(
        spread_kernel,
        out_shape=f32(X, COEFS, 8, cols),
        in_specs=[VMEM],
        out_specs=VMEM,
        compiler_params=SMALL,
        name="spread",
    )(coef.reshape(z * COEFS, 128))
    coef = lax.all_to_all(coef, "x", 0, 0, tiled=True)
    return pl.pallas_call(
        apply_kernel,
        out_shape=f32(LOCAL, FIELDS, rows, cols),
        in_specs=[VMEM] * 3,
        out_specs=VMEM,
        compiler_params=LARGE,
        name="apply",
    )(coef, inner_field, edge_field)


def solution(mesh):
    devices = mesh.devices
    fine = Mesh(devices.reshape(devices.shape[0] // X, X, devices.shape[1]), ("z", "x", "space"))
    member = ("z", "x")
    in_specs = (
        P(member, None, "space", None),
        P("space", None),
        P("space", None),
        P(None, "space", None),
        P(None, "space", None),
        P(None, "space", None),
        P(),
        P("space"),
    )
    out_specs = P(member, None, "space", None)
    return jax.shard_map(body, mesh=fine, in_specs=in_specs, out_specs=out_specs, check_vma=False)
```

```python
import functools

import jax
import jax.numpy as jnp
from jax import lax
from jax.experimental import pallas as pl
from jax.experimental.pallas import tpu as pltpu
from jax.sharding import Mesh, PartitionSpec as P

STEPS = 4
RADIUS = 4
LOCAL = 8
FIELDS = 3
X = 4
HALO = 8
STATS = 19
COEFS = 9

jitter = 0.05
pair_list = ((0, 0), (1, 0), (1, 1), (2, 0), (2, 1), (2, 2))
VMEM = pl.BlockSpec(memory_space=pltpu.VMEM)
HBM = pl.BlockSpec(memory_space=pltpu.HBM)

LARGE = pltpu.CompilerParams(vmem_limit_bytes=8 << 20)
SMALL = pltpu.CompilerParams(vmem_limit_bytes=2 << 20)


def cholesky_rows(matrix):
    first = jnp.sqrt(matrix[0])
    second = matrix[1] / first
    fourth = matrix[3] / first
    third = jnp.sqrt(matrix[2] - second * second)
    fifth = (matrix[4] - fourth * second) / third
    sixth = jnp.sqrt(matrix[5] - fourth * fourth - fifth * fifth)
    return [first, second, third, fourth, fifth, sixth]


def lower_inverse(packed):
    head = 1.0 / packed[0]
    middle = 1.0 / packed[2]
    tail = 1.0 / packed[5]
    below_head = -packed[1] * head * middle
    below_middle = -packed[4] * middle * tail
    corner = -(packed[3] * head + packed[4] * below_head) * tail
    return [head, below_head, middle, corner, below_middle, tail]


def lower_product(left_side, right_side):
    return [
        left_side[0] * right_side[0],
        left_side[1] * right_side[0] + left_side[2] * right_side[1],
        left_side[2] * right_side[2],
        left_side[3] * right_side[0] + left_side[4] * right_side[1] + left_side[5] * right_side[3],
        left_side[4] * right_side[2] + left_side[5] * right_side[4],
        left_side[5] * right_side[5],
    ]


HALF = 128
PAD = 8
TOGETHER = 8
MOVING = 8


def split(value):
    return value[:, :HALF], value[:, HALF:]


def lane_sides(pair, k):
    a, b = pair
    lane = lax.broadcasted_iota(jnp.int32, a.shape, 1)
    low, high = lane < k, lane >= HALF - k
    left_a, left_b = pltpu.roll(a, k, 1), pltpu.roll(b, k, 1)
    right_a, right_b = pltpu.roll(a, HALF - k, 1), pltpu.roll(b, HALF - k, 1)
    return (
        jnp.where(low, left_b, left_a) + jnp.where(high, right_b, right_a),
        jnp.where(low, left_a, left_b) + jnp.where(high, right_a, right_b),
    )


def advance(pairs, buffers, coef, trails):
    rows = pairs[0][0].shape[0]
    for step in range(STEPS):
        slots = [b.at[step % 2] for b in buffers]
        kept = slice(2 * step, 2 * step + 2)
        for slot, pair, trail in zip(slots, pairs, trails):
            for h in range(2):
                slot[h, PAD : PAD + rows] = pair[h]
                trail[0, h, kept] = slot[h, PAD + step : PAD + step + 2]
                trail[1, h, kept] = slot[h, PAD + rows - 2 - step : PAD + rows - step]
        after = []
        for slot, pair in zip(slots, pairs):
            sides = lane_sides(pair, 1)
            after.append(
                tuple(
                    coef[0, h] * pair[h]
                    + coef[1, h] * slot[h, PAD - 1 : PAD - 1 + rows]
                    + coef[2, h] * (slot[h, PAD + 1 : PAD + 1 + rows] + sides[h])
                    for h in range(2)
                )
            )
        pairs = after
    return pairs


def advance_windows(end, windows, buffers, coef, trails):
    for step in range(STEPS):
        slots = [b.at[step % 2] for b in buffers]
        kept = slice(2 * step, 2 * step + 2)
        for slot, window, trail in zip(slots, windows, trails):
            beside = PAD + 8 if end == 0 else PAD - 2
            for h in range(2):
                slot[h, PAD : PAD + 8] = window[h]
                slot[h, beside : beside + 2] = trail[end, h, kept]
        after = []
        for slot in slots:
            top = PAD if end == 0 else PAD - 2
            start = 1 + step if end == 0 else 7 - step
            center = tuple(slot[h, top + 1 : top + 9] for h in range(2))
            sides = lane_sides(center, 1)
            after.append(
                tuple(
                    coef[0, h, start : start + 8] * center[h]
                    + coef[1, h, start : start + 8] * slot[h, top : top + 8]
                    + coef[2, h, start : start + 8] * (slot[h, top + 2 : top + 10] + sides[h])
                    for h in range(2)
                )
            )
        windows = after
    return windows


def radius_weights(radii_ref, rows):
    radii = [jnp.concatenate([radii_ref[f]] * (rows // 8), axis=0) for f in range(FIELDS)]
    return [
        [None, None] + [jnp.where(r >= float(k), 1.0, 0.0) for k in range(2, RADIUS + 1)]
        for r in radii
    ]


def row_total(likelihood_ref, start, rows, weights):
    def both(k):
        return (
            likelihood_ref[start - k : start - k + rows]
            + likelihood_ref[start + k : start + k + rows]
        )

    outer = both(RADIUS)
    for k in range(RADIUS - 1, 0, -1):
        outer = both(k) + weights[k + 1] * outer
    return likelihood_ref[start : start + rows] + outer


def column_total(totals, weights):
    score = tuple(sum((t[h] for t in totals[1:]), totals[0][h]) for h in range(2))
    mixed = score
    for k in range(1, RADIUS + 1):
        if k > 1:
            totals = [
                tuple(weights[f][k] * t for t in totals[f]) for f in range(FIELDS)
            ]
            mixed = tuple(sum((t[h] for t in totals[1:]), totals[0][h]) for h in range(2))
        sides = lane_sides(mixed, k)
        score = tuple(score[h] + sides[h] for h in range(2))
    return score


def local_statistics(scores, cells):
    def plus(terms):
        return sum(terms[1:], terms[0])

    peak = scores[0]
    for s in scores[1:]:
        peak = jnp.maximum(peak, s)
    importance = [jnp.exp(s - peak) for s in scores]
    total = plus(importance)
    inverse = 1.0 / total
    share = 1.0 / LOCAL
    center = [plus([c[f] for c in cells]) * share for f in range(FIELDS)]
    away = [[c[f] - center[f] for f in range(FIELDS)] for c in cells]
    drift = [
        plus([w * a[f] for w, a in zip(importance, away)]) * inverse for f in range(FIELDS)
    ]
    post, prior = [], []
    for i, j in pair_list:
        products = [a[i] * a[j] for a in away]
        prior.append(plus(products) * share)
        post.append(
            plus([w * p for w, p in zip(importance, products)]) * inverse - drift[i] * drift[j]
        )
    moved = [center[f] + drift[f] for f in range(FIELDS)]
    return [peak + jnp.log(total)] + moved + post + center + prior


def pack_kernel(
    radius_hbm, temper_hbm, fields_hbm, spread_hbm, flow_hbm, quantity_hbm, confidence_hbm,
    mask_hbm, last_ref, leading_ref, par_ref, tempering_ref, radii_ref,
    radius_ref, temper_ref, confidence_ref, mask_ref, sems,
):
    planes, rows = fields_hbm.shape[:2]
    tail = pl.ds(rows - HALO, HALO)
    head = pl.ds(0, HALO)
    sent = pl.ds(0, planes)
    pairs = (
        (confidence_hbm, confidence_ref),
        (mask_hbm, mask_ref),
        (spread_hbm, par_ref.at[0]),
        (flow_hbm, par_ref.at[1]),
        (quantity_hbm, par_ref.at[pl.ds(2, FIELDS)]),
        (temper_hbm, temper_ref),
        (radius_hbm, radius_ref),
        (fields_hbm.at[:, tail], last_ref.at[sent]),
        (fields_hbm.at[:, head], leading_ref.at[sent]),
    )
    copies = [
        pltpu.make_async_copy(source, target, sems.at[number])
        for number, (source, target) in enumerate(pairs)
    ]
    for copy in copies:
        copy.start()
    for copy in copies[:7]:
        copy.wait()
    for f in range(FIELDS):
        par_ref[5 + f] = -0.5 * mask_ref[f].astype(jnp.float32) * confidence_ref[f]
        radius = radius_ref[:, f : f + 1].astype(jnp.float32)
        radii_ref[f] = jnp.broadcast_to(radius, (8, HALF))
    for out_ref, part, first in ((last_ref, tail, rows - 4), (leading_ref, head, 0)):
        for p in range(2):
            out_ref[planes + p] = par_ref[p, part]
        for f in range(FIELDS):
            out_ref[planes + 2 + f, 0:4] = par_ref[2 + f, first : first + 4]
            out_ref[planes + 2 + f, 4:8] = par_ref[5 + f, first : first + 4]
    row = lax.broadcasted_iota(jnp.int32, (rows, rows), 0)
    column = lax.broadcasted_iota(jnp.int32, (rows, rows), 1)
    along = jnp.broadcast_to(temper_ref[...].astype(jnp.float32), (rows, rows))
    each = jnp.sum(jnp.where(row == column, along, 0.0), axis=1, keepdims=True)
    tempering_ref[...] = jnp.exp2(-jnp.broadcast_to(each, (rows, HALF)))
    for copy in copies[7:]:
        copy.wait()


def interior_kernel(
    own_ref, par_ref, temper_ref, radii_ref, field_ref, stats_ref, trail_ref,
    coef_ref, buffer_ref, likelihood_ref, score_ref,
):
    rows = own_ref.shape[1]
    inner = rows - 16
    spread, flow = split(par_ref[0]), split(par_ref[1])
    for h in range(2):
        coef_ref[0, h] = 1.0 - 4.0 * spread[h] - flow[h]
        coef_ref[1, h] = spread[h] + flow[h]
        coef_ref[2, h] = spread[h]
    weights = radius_weights(radii_ref, inner)

    def some_members(step, carry):
        first = step * TOGETHER
        planes = range(TOGETHER * FIELDS)
        pairs = advance(
            [split(own_ref[first * FIELDS + p]) for p in planes],
            [buffer_ref.at[p] for p in planes],
            coef_ref,
            [trail_ref.at[first * FIELDS + p] for p in planes],
        )
        for p in planes:
            f = p % FIELDS
            quantity, observed = split(par_ref[2 + f]), split(par_ref[5 + f])
            for h in range(2):
                field_ref[first + p // FIELDS, f, h] = pairs[p][h]
                misfit = pairs[p][h] - quantity[h]
                likelihood_ref[p, h] = observed[h] * misfit * misfit
        for u in range(TOGETHER):
            totals = [
                tuple(
                    row_total(likelihood_ref.at[u * FIELDS + f, h], 8, inner, weights[f])
                    for h in range(2)
                )
                for f in range(FIELDS)
            ]
            score = column_total(totals, weights)
            for h in range(2):
                score_ref[first + u, h] = temper_ref[8 : 8 + inner] * score[h]
        return carry

    lax.fori_loop(0, LOCAL // TOGETHER, some_members, 0)

    def one_group(g, carry):
        sub = pl.ds(pl.multiple_of(g * 8, 8), 8)
        deep = pl.ds(pl.multiple_of(g * 8 + 8, 8), 8)
        for h in range(2):
            scores = [score_ref[m, h, sub] for m in range(LOCAL)]
            cells = [[field_ref[m, f, h, deep] for f in range(FIELDS)] for m in range(LOCAL)]
            for number, value in enumerate(local_statistics(scores, cells)):
                stats_ref[g, number, :, h * HALF : (h + 1) * HALF] = value
        return carry

    lax.fori_loop(0, inner // 8, one_group, 0)


def edge_kernel(end, trail_ref, halo_ref, own_par_ref, temper_ref, radii_ref, inner_field_ref, *refs):
    if end == 0:
        inner_stats_ref, last_stats_ref, *refs = refs
    field_ref, stats_ref, coef_ref, buffer_ref, par_ref, wide_ref, likelihood_ref, score_ref = refs
    rows = own_par_ref.shape[1]
    part = (slice(0, 8), slice(rows - 8, rows))[end]
    base = FIELDS * LOCAL
    if end == 0:
        for g in range(rows // 8 - 2):
            stats_ref[1 + g] = inner_stats_ref[g]
        stats_ref[rows // 8 - 1] = last_stats_ref[0]

    def framed(own, halo):
        return jnp.concatenate([halo, own] if end == 0 else [own, halo], axis=0)

    spread = split(framed(own_par_ref[0, part], halo_ref[base]))
    flow = split(framed(own_par_ref[1, part], halo_ref[base + 1]))
    for h in range(2):
        coef_ref[0, h] = 1.0 - 4.0 * spread[h] - flow[h]
        coef_ref[1, h] = spread[h] + flow[h]
        coef_ref[2, h] = spread[h]
    outer, inner = (slice(4, 8), slice(8, 24)) if end == 0 else (slice(16, 20), slice(0, 16))
    own_rows = slice(0, 16) if end == 0 else slice(rows - 16, rows)
    for p in range(6):
        half_plane = slice(0, 4) if p < FIELDS else slice(4, 8)
        for h in range(2):
            lane = slice(h * HALF, (h + 1) * HALF)
            par_ref[p, h, outer] = halo_ref[base + 2 + p % FIELDS, half_plane, lane]
            par_ref[p, h, inner] = own_par_ref[2 + p, own_rows, lane]
    counted = slice(4, 20)
    weights = radius_weights(radii_ref, 8)

    def some_members(step, carry):
        first = step * TOGETHER
        planes = range(TOGETHER * FIELDS)
        pairs = advance_windows(
            end,
            [split(halo_ref[first * FIELDS + p]) for p in planes],
            [buffer_ref.at[p] for p in planes],
            coef_ref,
            [trail_ref.at[first * FIELDS + p] for p in planes],
        )
        for p, pair in zip(planes, pairs):
            m, f = first + p // FIELDS, p % FIELDS
            for h in range(2):
                wide = wide_ref.at[p, h]
                new = pair[h]
                old = inner_field_ref[m, f, h, (4, rows - 12)[end] : (12, rows - 4)[end]]
                wide[0:8] = (new, old)[end]
                wide[8:16] = (old, new)[end]
                field_ref[m, f, h] = wide[4:12]
                misfit = framed(old, new) - par_ref[f, h, counted]
                likelihood_ref[p, h] = par_ref[3 + f, h, counted] * misfit * misfit
        for u in range(TOGETHER):
            totals = [
                tuple(
                    row_total(likelihood_ref.at[u * FIELDS + f, h], 4, 8, weights[f])
                    for h in range(2)
                )
                for f in range(FIELDS)
            ]
            score = column_total(totals, weights)
            for h in range(2):
                score_ref[first + u, h] = temper_ref[part] * score[h]
        return carry

    lax.fori_loop(0, LOCAL // TOGETHER, some_members, 0)

    for h in range(2):
        scores = [score_ref[m, h] for m in range(LOCAL)]
        cells = [[field_ref[m, f, h] for f in range(FIELDS)] for m in range(LOCAL)]
        for number, value in enumerate(local_statistics(scores, cells)):
            stats_ref[0, number, :, h * HALF : (h + 1) * HALF] = value


def merged(parts, add, biggest):
    peak = biggest(parts[0])
    mass = [jnp.exp(p - peak) for p in parts[0]]
    total = add(mass)
    out = [peak + jnp.log(total)]
    for first, weights in ((1, mass), (10, None)):
        count = len(mass)

        def average(terms):
            if weights is None:
                return add(terms)
            return add([weights[s] * terms[s] for s in range(count)])

        share = 1.0 / (total if weights is not None else add([jnp.ones_like(m) for m in mass]))
        means = [average(parts[first + f]) * share for f in range(FIELDS)]
        away = [[parts[first + f][s] - means[f] for s in range(count)] for f in range(FIELDS)]
        out += means
        for number, (i, j) in enumerate(pair_list):
            second = parts[first + FIELDS + number]
            out.append(
                average([second[s] + away[i][s] * away[j][s] for s in range(count)]) * share
            )
    return out


def merge_x_kernel(part_ref, out_ref):
    def add(terms):
        return sum(terms[1:], terms[0])

    def biggest(terms):
        peak = terms[0]
        for t in terms[1:]:
            peak = jnp.maximum(peak, t)
        return peak

    for half in range(2):
        lane = pl.ds(half * 128, 128)
        parts = [[part_ref[s, p, :, lane] for s in range(X)] for p in range(STATS)]
        out = merged(parts, add, biggest)
        for p in range(STATS):
            out_ref[pl.ds(half * 8 * STATS + p, 8, stride=STATS), :] = out[p]


def merge_z_kernel(part_ref, out_ref):
    sources = part_ref.shape[0] // STATS
    blocks = sources // 8

    def add(terms):
        return jnp.sum(sum(terms[1:], terms[0]), axis=0, keepdims=True)

    def biggest(terms):
        peak = terms[0]
        for t in terms[1:]:
            peak = jnp.maximum(peak, t)
        return jnp.max(peak, axis=0, keepdims=True)

    parts = [
        [part_ref[pl.ds(b * 8 * STATS + p, 8, stride=STATS), :] for b in range(blocks)]
        for p in range(STATS)
    ]
    out = merged(parts, add, biggest)
    diagonal = (0, 2, 5)
    post_cov = [out[4 + n] + (jitter if n in diagonal else 0.0) for n in range(6)]
    prior_cov = [out[13 + n] + (jitter if n in diagonal else 0.0) for n in range(6)]
    gain = lower_product(cholesky_rows(post_cov), lower_inverse(cholesky_rows(prior_cov)))
    result = list(gain)
    for row in range(FIELDS):
        running = out[1 + row]
        for source in range(row + 1):
            running = running - gain[row * (row + 1) // 2 + source] * out[10 + source]
        result.append(running)
    for p in range(COEFS):
        value = jnp.broadcast_to(result[p], (8, 128))
        for b in range(blocks):
            out_ref[pl.ds(b * 8 * COEFS + p, 8, stride=COEFS), :] = value


def spread_kernel(coef_ref, out_ref):
    for half in range(2):
        lane = pl.ds(half * HALF, HALF)
        for p in range(COEFS):
            value = coef_ref[pl.ds(half * 8 * COEFS + p, 8, stride=COEFS), :]
            for target in range(X):
                out_ref[target, p, :, lane] = value


def apply_kernel(coef_ref, inner_ref, first_ref, last_ref, out_ref):
    last = X - 1

    def one_member(m, carry):
        for g in range(X):
            for h in range(2):
                lane = slice(h * HALF, (h + 1) * HALF)
                if g in (0, last):
                    edge_ref = first_ref if g == 0 else last_ref
                    cells = [edge_ref[m, f, h] for f in range(FIELDS)]
                else:
                    cells = [inner_ref[m, f, h, g * 8 : g * 8 + 8] for f in range(FIELDS)]
                for row in range(FIELDS):
                    running = coef_ref[g, 6 + row, :, lane]
                    for source in range(row + 1):
                        entry = coef_ref[g, row * (row + 1) // 2 + source, :, lane]
                        running = running + entry * cells[source]
                    out_ref[m, row, g * 8 : g * 8 + 8, lane] = running
        return carry

    lax.fori_loop(0, LOCAL, one_member, 0)


def f32(*shape):
    return jax.ShapeDtypeStruct(shape, jnp.float32)


def body(
    sample_group,
    spreading_ratio,
    flow_ratio,
    measured_quantity,
    measured_confidence,
    obs_mask,
    radius,
    temper,
):
    rows, cols = sample_group.shape[2:]
    z = lax.axis_size("z")
    sent = LOCAL * FIELDS + 2 + FIELDS
    planes = sample_group.reshape(LOCAL * FIELDS, rows, cols)
    last, leading, own_par, tempering, radii = pl.pallas_call(
        pack_kernel,
        out_shape=(
            f32(sent, HALO, cols),
            f32(sent, HALO, cols),
            f32(MOVING, rows, cols),
            f32(rows, HALF),
            f32(FIELDS, 8, HALF),
        ),
        in_specs=[HBM] * 8,
        out_specs=(VMEM,) * 5,
        scratch_shapes=[
            pltpu.VMEM((1, FIELDS), jnp.int32),
            pltpu.VMEM((1, rows), jnp.int32),
            pltpu.VMEM((FIELDS, rows, cols), jnp.float32),
            pltpu.VMEM((FIELDS, rows, cols), jnp.int32),
            pltpu.SemaphoreType.DMA((9,)),
        ],
        compiler_params=LARGE,
        name="pack",
    )(
        *(
            pltpu.with_memory_space_constraint(array, pltpu.HBM)
            for array in (
                radius.reshape(1, FIELDS),
                temper.reshape(1, rows),
                planes,
                spreading_ratio,
                flow_ratio,
                measured_quantity,
                measured_confidence,
                obs_mask,
            )
        )
    )
    count = lax.axis_size("space")
    up = [(i, (i + 1) % count) for i in range(count)]
    down = [(j, i) for i, j in up]
    above = lax.ppermute(last, "space", up)
    below = lax.ppermute(leading, "space", down)
    inner_field, inner_stats, trail = pl.pallas_call(
        interior_kernel,
        out_shape=(
            f32(LOCAL, FIELDS, 2, rows, HALF),
            f32(rows // 8 - 2, STATS, 8, cols),
            f32(LOCAL * FIELDS, 2, 2, 2 * STEPS, HALF),
        ),
        in_specs=[VMEM] * 4,
        out_specs=(VMEM,) * 3,
        scratch_shapes=[
            pltpu.VMEM((3, 2, rows, HALF), jnp.float32),
            pltpu.VMEM((TOGETHER * FIELDS, 2, 2, rows + 2 * PAD, HALF), jnp.float32),
            pltpu.VMEM((TOGETHER * FIELDS, 2, rows, HALF), jnp.float32),
            pltpu.VMEM((LOCAL, 2, rows - 16, HALF), jnp.float32),
        ],
        compiler_params=LARGE,
        name="interior",
    )(planes, own_par, tempering, radii)

    def edge(end, halo, *stats):
        return pl.pallas_call(
            functools.partial(edge_kernel, end),
            out_shape=(
                f32(LOCAL, FIELDS, 2, 8, HALF),
                f32(X if end == 0 else 1, STATS, 8, cols),
            ),
            in_specs=[VMEM] * (6 + len(stats)),
            out_specs=(VMEM, VMEM),
            scratch_shapes=[
                pltpu.VMEM((3, 2, 16, HALF), jnp.float32),
                pltpu.VMEM((TOGETHER * FIELDS, 2, 2, 8 + 2 * PAD, HALF), jnp.float32),
                pltpu.VMEM((6, 2, 24, HALF), jnp.float32),
                pltpu.VMEM((TOGETHER * FIELDS, 2, 16, HALF), jnp.float32),
                pltpu.VMEM((TOGETHER * FIELDS, 2, 16, HALF), jnp.float32),
                pltpu.VMEM((LOCAL, 2, 8, HALF), jnp.float32),
            ],
            compiler_params=LARGE,
            name=f"edge{end}",
        )(trail, halo, own_par, tempering, radii, inner_field, *stats)

    last_field, last_stats = edge(1, below)
    first_field, stats = edge(0, above, inner_stats, last_stats)

    stats = lax.all_to_all(stats, "x", 0, 0, tiled=True)
    stats = pl.pallas_call(
        merge_x_kernel,
        out_shape=f32(z * STATS, 128),
        in_specs=[VMEM],
        out_specs=VMEM,
        compiler_params=SMALL,
        name="merge_x",
    )(stats)
    stats = lax.all_to_all(stats.reshape(z, STATS, 1, 128), "z", 0, 0, tiled=True)
    coef = pl.pallas_call(
        merge_z_kernel,
        out_shape=f32(z * COEFS, 128),
        in_specs=[VMEM],
        out_specs=VMEM,
        compiler_params=SMALL,
        name="merge_z",
    )(stats.reshape(z * STATS, 128))
    coef = lax.all_to_all(coef.reshape(z, COEFS, 1, 128), "z", 0, 0, tiled=True)
    coef = pl.pallas_call(
        spread_kernel,
        out_shape=f32(X, COEFS, 8, cols),
        in_specs=[VMEM],
        out_specs=VMEM,
        compiler_params=SMALL,
        name="spread",
    )(coef.reshape(z * COEFS, 128))
    coef = lax.all_to_all(coef, "x", 0, 0, tiled=True)
    return pl.pallas_call(
        apply_kernel,
        out_shape=f32(LOCAL, FIELDS, rows, cols),
        in_specs=[VMEM] * 4,
        out_specs=VMEM,
        compiler_params=LARGE,
        name="apply",
    )(coef, inner_field, first_field, last_field)


def solution(mesh):
    devices = mesh.devices
    fine = Mesh(devices.reshape(devices.shape[0] // X, X, devices.shape[1]), ("z", "x", "space"))
    member = ("z", "x")
    in_specs = (
        P(member, None, "space", None),
        P("space", None),
        P("space", None),
        P(None, "space", None),
        P(None, "space", None),
        P(None, "space", None),
        P(),
        P("space"),
    )
    out_specs = P(member, None, "space", None)
    return jax.shard_map(body, mesh=fine, in_specs=in_specs, out_specs=out_specs, check_vma=False)
```
